256 devices in a mesh: dp: 8 (over x, core), expert: 32 (over z, y).
Axes of the slice: x: 4, y: 4, z: 8, core: 2. Of those that a mesh axis runs over, the one named last changes fastest.
Arguments:
- tokens: bfloat16 [4096, 2048], P('expert', 'dp'), may hold values from -6 to 6
- cotangent: bfloat16 [4096, 2048], P('expert', 'dp'), may hold values from -6 to 6
- route: int32 [4096, 8], P('expert'), may hold values from 0 to 95, all different within a row; in each aligned block of 128 rows (0 to 127, 128 to 255, ...) at most 12 rows name the same one
- gate_prob: float32 [4096, 8], P('expert'), may hold values from 0.02 to 0.25
- replica_pick: int32 [32], replicated, may hold values from 0 to 1
- w_gate: bfloat16 [64, 1536, 2048], P('expert', 'dp'), may hold values from -0.125 to 0.125
- w_up: bfloat16 [64, 1536, 2048], P('expert', 'dp'), may hold values from -0.125 to 0.125
- w_down: bfloat16 [64, 1536, 2048], P('expert', 'dp'), may hold values from -0.15625 to 0.15625
Outputs:
- layer_out: bfloat16 [4096, 2048], P('expert', 'dp')
- token_grad: bfloat16 [4096, 2048], P('expert', 'dp')
- gate_grad: float32 [4096, 8], P('expert', 'dp')
- w_gate_grad: bfloat16 [64, 1536, 2048], P('expert', 'dp')
- w_up_grad: bfloat16 [64, 1536, 2048], P('expert', 'dp')
- w_down_grad: bfloat16 [64, 1536, 2048], P('expert', 'dp')
The draws below stay inside these ranges and needn't reach their ends.
Inputs may be any that keep to these rules, and one draw needn't show every extreme that they name: `route`: each row names 8 different copies. Among the rows of one device, in aligned blocks of 128 tokens, no copy is named more than 12 times, a bound that some block reaches.
All inputs are finite; a program needn't handle non-finite values.
Results may differ from the reference program's by a relative error of at most 0.014.
Values may be sent and summed in bfloat16 or wider, within the bound.
No kernel may reach another device: no remote copies, remote signals or barrier semaphores. Data moves between devices by JAX's collectives and lax.ppermute only.
A program may use at most 128 MiB of HBM per device.

```python
import math
import jax
import jax.numpy as jnp
import numpy as np
from jax import lax

D = 2048
FF = 1536
TOP = 8
EXP_DEV = 2
TOK_DEV = 128
EXPERTS = 64
TOKENS = 4096
FF_DEV = 192
COPIES = 96
CAP = 12
N_DP = 8
N_EXPERT = 32


def with_ends(result, own_key, low, top_value):
    index_at = [jax.random.randint(jax.random.fold_in(own_key, axis), (), 0, length) for axis, length in enumerate(result.shape)]
    widest = result.shape.index(max(result.shape))
    beside = index_at[:widest] + [(index_at[widest] + 1) % result.shape[widest]] + index_at[widest + 1:]
    return result.at[tuple(index_at)].set(low).at[tuple(beside)].set(top_value)


def level_of(rng, extent, cuts, low, top_value):
    def one(dim, parts):
        draws = jax.random.uniform(jax.random.fold_in(jax.random.fold_in(rng, 6), dim), (parts,), jnp.float32, low / len(cuts), top_value / len(cuts))
        return jnp.repeat(jnp.exp(draws), extent[dim] // parts).reshape((-1,) + (1,) * (len(extent) - dim - 1))

    loudness = one(*cuts[0])
    for cut in cuts[1:]:
        loudness = loudness * one(*cut)
    return loudness


def shared_out(key, own, number, rows, number_of, top, most, skew):
    sequence = jax.random.permutation(key, number_of)
    crowded, usual = portions_of(number_of, rows * top, most, skew, True), portions_of(number_of, rows * top, most, skew, False)
    places = jnp.arange(number_of)

    def named(lengths, turn):
        used = int((lengths > 0).sum())
        fixed = max(1, used // 4)
        shifted = fixed + (places - fixed + turn * (used - fixed)) % max(1, number_of - fixed)
        return jnp.zeros((number_of,), jnp.int32).at[sequence[jnp.where(places < fixed, places, shifted)]].set(jnp.asarray(lengths, jnp.int32))

    lengths = jnp.where(number % 4 == 0, named(crowded, number // 4), named(usual, number - number // 4 - 1))
    mixed = jax.random.permutation(jax.random.fold_in(own, 3), number_of)
    source_of, receiver = mixed[0:number_of // 2 * 2:2], mixed[1:number_of // 2 * 2:2]
    margin = jnp.minimum(lengths[source_of] - 1, most - lengths[receiver]) // 2
    margin = jnp.where((source_of == sequence[0]) | (receiver == sequence[0]) | (lengths[receiver] == 0), 0, jnp.maximum(margin, 0))
    shifted = jax.random.randint(jax.random.fold_in(own, 4), (number_of // 2,), 0, 1 << 20) % (margin + 1)
    lengths = lengths.at[source_of].add(-shifted).at[receiver].add(shifted)
    labels = jnp.searchsorted(jnp.cumsum(lengths), jnp.arange(rows * top), side="right").astype(jnp.int32)
    listing = labels.reshape(top, rows).T
    listing = listing[jax.random.permutation(jax.random.fold_in(own, 1), rows)]
    turn = jax.random.randint(jax.random.fold_in(own, 2), (rows, 1), 0, top)
    return jnp.take_along_axis(listing, (jnp.arange(top)[None, :] + turn) % top, axis=1)


def portions_of(number_of, total, limit, skew, full):
    portions = [(1 << 20) // math.isqrt(grade ** skew) + 1 for grade in range(1, number_of + 1)]
    largest = limit if full else min(limit, max(-(-total // number_of), total * portions[0] // sum(portions)))
    least = 1 if total - largest >= number_of - 1 else 0
    holding, surplus = [largest] + [least] * (number_of - 1), total - largest - least * (number_of - 1)
    while surplus > 0:
        free = [i for i in range(1, number_of) if holding[i] < largest] or [i for i in range(1, number_of) if holding[i] < limit]
        mass, budget = sum([portions[i] for i in free]), surplus
        for i in free:
            addition = min(limit - holding[i], max(1, budget * portions[i] // mass), surplus)
            holding[i] = holding[i] + addition
            surplus = surplus - addition
    return np.array(holding)


def noise(own_key, shape, spread, limit, shards=(), kind=jnp.bfloat16):
    factor_of = level_of(own_key, shape, shards, -0.22, 0.18) if shards else 1.0
    entries = jax.random.normal(own_key, shape, jnp.float32) * spread * factor_of
    return jnp.minimum(jnp.maximum(entries, -limit), limit).astype(kind)


def setup_inputs(seed: int = 0) -> dict:
    seeds = jax.random.split(jax.random.key(seed), 9)
    tokens = noise(seeds[0], (TOKENS, D), 1.0, 6.0, ((0, 32), (1, 8)))
    cotangent = noise(seeds[1], (TOKENS, D), 1.0, 6.0, ((0, 32), (1, 8)))
    route_keys = jax.random.split(jax.random.fold_in(seeds[2], 1), TOKENS // TOK_DEV)
    route_turns = jax.random.permutation(jax.random.fold_in(seeds[2], 3), TOKENS // TOK_DEV)
    route = jax.vmap(lambda own, number: shared_out(jax.random.fold_in(seeds[2], 2), own, number, TOK_DEV, COPIES, TOP, CAP, 2))(route_keys, route_turns).reshape((TOKENS, TOP))
    gate_prob = jnp.clip(0.02 + 0.23 * jax.random.uniform(seeds[3], (TOKENS, TOP), jnp.float32) ** level_of(seeds[3], (TOKENS, TOP), ((0, 32),), -0.2, 0.2), 0.02, 0.25)
    replica_pick = with_ends(jax.random.randint(seeds[4], (N_EXPERT,), 0, EXP_DEV), jax.random.fold_in(seeds[4], 1), 0, EXP_DEV - 1).astype(jnp.int32)
    w_gate = noise(seeds[5], (EXPERTS, FF, D), D ** -0.5, 0.125, ((0, 32), (1, 8)))
    w_up = noise(seeds[6], (EXPERTS, FF, D), D ** -0.5, 0.125, ((0, 32), (1, 8)))
    w_down = noise(seeds[7], (EXPERTS, FF, D), FF ** -0.5, 0.15625, ((0, 32), (1, 8)))
    return dict(tokens=tokens, cotangent=cotangent, route=route, gate_prob=gate_prob, replica_pick=replica_pick, w_gate=w_gate, w_up=w_up, w_down=w_down)


def rounded_f32(values):
    return lax.optimization_barrier(values.astype(jnp.bfloat16)).astype(jnp.float32)


def reference(tokens, cotangent, route, gate_prob, replica_pick, w_gate, w_up, w_down):
    local_copies = EXP_DEV + 1
    slots = TOKENS * TOP
    route_rows = route.reshape(N_EXPERT, TOK_DEV * TOP)
    onehot = (route_rows[:, :, None] == jnp.arange(COPIES, dtype=jnp.int32)[None, None, :]).astype(jnp.int32)
    position = jnp.sum((jnp.cumsum(onehot, axis=1) - 1) * onehot, axis=2).astype(jnp.int32)
    source = jnp.arange(N_EXPERT, dtype=jnp.int32)[:, None]
    address = ((route_rows * N_EXPERT + source) * CAP + position).reshape(-1).astype(jnp.int32)
    slot_table = jnp.full((COPIES * N_EXPERT * CAP,), slots, jnp.int32).at[address].set(jnp.arange(slots, dtype=jnp.int32))
    slot_table = slot_table.reshape(COPIES, N_EXPERT * CAP)
    pad_tokens = jnp.concatenate([tokens, jnp.zeros((1, D), tokens.dtype)], axis=0)
    pad_cot = jnp.concatenate([cotangent, jnp.zeros((1, D), cotangent.dtype)], axis=0)
    pad_gate = jnp.concatenate([gate_prob.reshape(-1), jnp.zeros((1,), gate_prob.dtype)], axis=0)
    rows_per = N_EXPERT * CAP

    def owner_step(carry, owner_col):
        out_acc, back_acc, prob_acc = carry
        partner = (owner_col + N_EXPERT // 2) % N_EXPERT
        own_list = owner_col * local_copies + jnp.arange(EXP_DEV, dtype=jnp.int32)
        guest_copy = partner * local_copies + EXP_DEV
        copy_list = jnp.concatenate([own_list, guest_copy[None]]).astype(jnp.int32)
        slot_ids = slot_table[copy_list]
        chosen_index = replica_pick[partner]
        start = (owner_col * EXP_DEV).astype(jnp.int32)

        def stacked(weights):
            owned_w = lax.dynamic_slice_in_dim(weights, start, EXP_DEV, 0)
            extra_w = lax.dynamic_index_in_dim(owned_w, chosen_index, 0, keepdims=True)
            return jnp.concatenate([owned_w, extra_w], axis=0).astype(jnp.float32)

        gate_w = stacked(w_gate)
        up_w = stacked(w_up)
        down_w = stacked(w_down)
        token_ids = slot_ids // TOP
        rows_in = pad_tokens[token_ids].astype(jnp.float32)
        gates = pad_gate[slot_ids].astype(jnp.float32)
        rows_dy = pad_cot[token_ids].astype(jnp.float32)
        rows_cot = (gates[..., None] * rows_dy).astype(jnp.bfloat16).astype(jnp.float32)
        gate_act = jnp.einsum("cmd,cfd->cmf", rows_in, gate_w)
        up_act = jnp.einsum("cmd,cfd->cmf", rows_in, up_w)
        sigmoid_gate = jax.nn.sigmoid(gate_act)
        activated = gate_act * sigmoid_gate
        hidden = (activated * up_act).astype(jnp.bfloat16).astype(jnp.float32)
        blocks = (local_copies, N_DP, FF_DEV, D)
        hidden_blocks = hidden.reshape(local_copies, rows_per, N_DP, FF_DEV)
        out_sum = jnp.sum(rounded_f32(jnp.einsum("cmrf,crfd->crmd", hidden_blocks, down_w.reshape(blocks))), axis=1)
        d_hidden = jnp.einsum("cmd,cfd->cmf", rows_cot, down_w)
        d_gate = (d_hidden * up_act * sigmoid_gate * (1.0 + gate_act * (1.0 - sigmoid_gate))).astype(jnp.bfloat16).astype(jnp.float32)
        d_up = (d_hidden * activated).astype(jnp.bfloat16).astype(jnp.float32)
        back_blocks = jnp.einsum("cmrf,crfd->crmd", d_gate.reshape(local_copies, rows_per, N_DP, FF_DEV), gate_w.reshape(blocks))
        back_blocks = back_blocks + jnp.einsum("cmrf,crfd->crmd", d_up.reshape(local_copies, rows_per, N_DP, FF_DEV), up_w.reshape(blocks))
        back_sum = jnp.sum(rounded_f32(back_blocks), axis=1)
        grad_gate = jnp.einsum("cmf,cmd->cfd", d_gate, rows_in)
        grad_up = jnp.einsum("cmf,cmd->cfd", d_up, rows_in)
        grad_down = jnp.einsum("cmf,cmd->cfd", hidden, rows_cot)
        select = (jnp.arange(EXP_DEV, dtype=jnp.int32) == chosen_index).astype(jnp.float32)[:, None, None]
        out_gate = (grad_gate[:EXP_DEV] + select * grad_gate[EXP_DEV]).astype(jnp.bfloat16)
        out_up = (grad_up[:EXP_DEV] + select * grad_up[EXP_DEV]).astype(jnp.bfloat16)
        out_down = (grad_down[:EXP_DEV] + select * grad_down[EXP_DEV]).astype(jnp.bfloat16)
        flat_tok = token_ids.reshape(-1)
        flat_slot = slot_ids.reshape(-1)
        out_acc = out_acc.at[flat_tok].add((gates[..., None] * out_sum).reshape(-1, D))
        back_acc = back_acc.at[flat_tok].add(back_sum.reshape(-1, D))
        prob_acc = prob_acc.at[flat_slot].set(jnp.sum(rows_dy * out_sum, axis=-1).reshape(-1))
        return (out_acc, back_acc, prob_acc), (out_gate, out_up, out_down)

    start_carry = (jnp.zeros((TOKENS + 1, D), jnp.float32), jnp.zeros((TOKENS + 1, D), jnp.float32), jnp.zeros((slots + 1,), jnp.float32))
    final, grads = lax.scan(owner_step, start_carry, jnp.arange(N_EXPERT, dtype=jnp.int32))
    out_acc, back_acc, prob_acc = final
    layer_out = out_acc[:TOKENS].astype(jnp.bfloat16)
    token_grad = back_acc[:TOKENS].astype(jnp.bfloat16)
    gate_grad = prob_acc[:slots].reshape(TOKENS, TOP)
    w_gate_grad = grads[0].reshape(EXPERTS, FF, D)
    w_up_grad = grads[1].reshape(EXPERTS, FF, D)
    w_down_grad = grads[2].reshape(EXPERTS, FF, D)
    return (layer_out, token_grad, gate_grad, w_gate_grad, w_up_grad, w_down_grad)
```

```python
import functools

import jax
import jax.numpy as jnp
from jax import lax
from jax.experimental import pallas as pl
from jax.sharding import PartitionSpec as P

BF = jnp.bfloat16
F32 = jnp.float32


def row_codes(first, rows, tok_dev, part, groups, owned, capacity):
    local_copies = owned + 1
    r = first + lax.broadcasted_iota(jnp.int32, (rows, tok_dev), 0)
    wide = 2 * capacity
    group = (r.astype(F32) * (1.0 / wide) + 0.5 / wide).astype(jnp.int32)
    inside = r - group * wide
    front = inside < capacity
    place = jnp.where(front, inside, inside - capacity)
    if part < owned:
        copy = group * local_copies + part
    else:
        holder = group + groups // 2
        holder = jnp.where(holder >= groups, holder - groups, holder)
        copy = holder * local_copies + owned
    return copy * capacity + place, front


def send_kernel(owned, groups, capacity, block, route_ref, gate_ref, tok_ref, cot_ref, code_ref, *out_refs):
    fanout, tok_dev = route_ref.shape
    copies = groups * (owned + 1)
    ids = lax.broadcasted_iota(jnp.int32, (copies, tok_dev), 0)
    named = jnp.zeros((copies, tok_dev), F32)
    for k in range(fanout):
        named = jnp.where(route_ref[k : k + 1, :] == ids, 1.0, named)
    before = lax.broadcasted_iota(jnp.int32, (tok_dev, tok_dev), 0) < lax.broadcasted_iota(
        jnp.int32, (tok_dev, tok_dev), 1
    )
    rank = jnp.dot(named.astype(BF), jnp.where(before, 1.0, 0.0).astype(BF), preferred_element_type=F32)
    codes, gates = [], []
    for k in range(fanout):
        row = route_ref[k : k + 1, :]
        at = jnp.sum(jnp.where(row == ids, rank, 0.0), axis=0, keepdims=True)
        codes.append(row * capacity + at.astype(jnp.int32))
        gates.append(gate_ref[k : k + 1, :])
    code_ref[...] = jnp.concatenate(codes, axis=0)
    both = jnp.concatenate([tok_ref[...], cot_ref[...]], axis=0)
    for part, out_ref in enumerate(out_refs):
        for first in range(0, out_ref.shape[0], block):
            slot, front = row_codes(first, block, tok_dev, part, groups, owned, capacity)
            match = jnp.zeros((block, tok_dev), F32)
            scale = jnp.zeros((block, tok_dev), F32)
            for k in range(fanout):
                same = codes[k] == slot
                match = jnp.where(same, 1.0, match)
                scale = jnp.where(same, gates[k], scale)
            pick = jnp.concatenate([jnp.where(front, match, 0.0), jnp.where(front, 0.0, match)], axis=1)
            rows = jnp.dot(pick.astype(BF), both, preferred_element_type=F32)
            scale = jnp.sum(jnp.where(front, 0.0, scale), axis=1, keepdims=True)
            scale = jnp.where(front[:, :1], 1.0, scale)
            out_ref[first : first + block, :] = (rows * scale).astype(BF)


def send_rows(route_t, gate_t, tokens, cot, owned, groups, capacity):
    rows, width = groups * 2 * capacity, tokens.shape[1]
    out = pl.pallas_call(
        functools.partial(send_kernel, owned, groups, capacity, 4 * 2 * capacity),
        out_shape=[jax.ShapeDtypeStruct(route_t.shape, jnp.int32)]
        + [jax.ShapeDtypeStruct((rows, width), BF)] * (owned + 1),
        name="send_rows",
    )(route_t, gate_t, tokens, cot)
    return out[0], out[1:]


def combine_kernel(owned, groups, capacity, part, first_call, last_call, *refs):
    code_ref, gate_ref, cot_ref, got_ref = refs[:4]
    acc_ref, gp_ref = (None, None) if first_call else refs[4:6]
    outs = refs[4:] if first_call else refs[6:]
    fanout, tok_dev = code_ref.shape
    got = got_ref[...]
    nt = (((1,), (1,)), ((), ()))
    tn = (((0,), (0,)), ((), ()))
    z = lax.dot_general(got, cot_ref[...], nt, preferred_element_type=F32)
    slot, front = row_codes(0, got.shape[0], tok_dev, part, groups, owned, capacity)
    match = jnp.zeros(z.shape, F32)
    scale = jnp.zeros(z.shape, F32)
    zf = jnp.where(front, z, 0.0)
    parts = []
    for k in range(fanout):
        same = code_ref[k : k + 1, :] == slot
        match = jnp.where(same, 1.0, match)
        scale = jnp.where(same, gate_ref[k : k + 1, :], scale)
        parts.append(jnp.sum(jnp.where(same, zf, 0.0), axis=0, keepdims=True))
    scale = jnp.where(front, scale, 0.0)
    high = scale.astype(BF)
    low = (scale - high.astype(F32)).astype(BF)
    back = jnp.where(front, 0.0, match).astype(BF)
    weights = jnp.concatenate([high, low, back], axis=1)
    acc = lax.dot_general(weights, got, tn, preferred_element_type=F32)
    gp = jnp.concatenate(parts, axis=0)
    if not first_call:
        acc = acc + acc_ref[...]
        gp = gp + gp_ref[...]
    if last_call:
        outs[0][...] = (acc[:tok_dev] + acc[tok_dev : 2 * tok_dev]).astype(BF)
        outs[1][...] = acc[2 * tok_dev :].astype(BF)
        outs[2][...] = gp
    else:
        outs[0][...] = acc
        outs[1][...] = gp


def combine(code, gate_t, cot, got, carried, part, last_call, owned, groups, capacity):
    tok_dev, width = cot.shape
    gp_shape = jax.ShapeDtypeStruct(code.shape, F32)
    if last_call:
        out_shape = [jax.ShapeDtypeStruct((tok_dev, width), BF)] * 2 + [gp_shape]
    else:
        out_shape = [jax.ShapeDtypeStruct((3 * tok_dev, width), F32), gp_shape]
    return pl.pallas_call(
        functools.partial(combine_kernel, owned, groups, capacity, part, not carried, last_call),
        out_shape=out_shape,
        name=f"combine_{part}",
    )(code, gate_t, cot, got, *carried)


def expert_math(rows_in, rows_cot, gate_w, up_w, down_w):
    def wide(x, w):
        return jnp.einsum("md,fd->mf", x, w, preferred_element_type=F32)

    gate_act, up_act, d_hidden = wide(rows_in, gate_w), wide(rows_in, up_w), wide(rows_cot, down_w)
    sigmoid_gate = jax.nn.sigmoid(gate_act)
    activated = gate_act * sigmoid_gate
    hidden = (activated * up_act).astype(BF)
    d_gate = (d_hidden * up_act * sigmoid_gate * (1.0 + gate_act * (1.0 - sigmoid_gate))).astype(BF)
    d_up = (d_hidden * activated).astype(BF)
    out_rows = jnp.einsum("mf,fd->md", hidden, down_w, preferred_element_type=F32)
    back_rows = jnp.einsum("mf,fd->md", d_gate, gate_w, preferred_element_type=F32)
    back_rows = back_rows + jnp.einsum("mf,fd->md", d_up, up_w, preferred_element_type=F32)
    return hidden, d_gate, d_up, jnp.stack([out_rows.astype(BF), back_rows.astype(BF)])


def body(tokens, cotangent, route, gate_prob, replica_pick, w_gate, w_up, w_down):
    groups = lax.axis_size("expert")
    column = lax.axis_index("expert")
    tok_dev, width = tokens.shape
    fanout = route.shape[1]
    owned = w_gate.shape[0]
    local_copies = owned + 1
    capacity = tok_dev * fanout // (groups * local_copies) + 2
    sizes = (owned, groups, capacity)
    rows = groups * capacity
    route_t, gate_t = route.T, gate_prob.T
    code, sends = send_rows(route_t, gate_t, tokens, cotangent, *sizes)

    own_pick = replica_pick[(column + groups // 2) % groups]
    weights = [(w_gate[i], w_up[i], w_down[i]) for i in range(owned)]
    weights.append(
        tuple(lax.dynamic_index_in_dim(w, own_pick, 0, keepdims=False) for w in (w_gate, w_up, w_down))
    )

    def swap(x):
        return lax.all_to_all(x.reshape(groups, 2 * capacity, width), "expert", split_axis=0, concat_axis=0, tiled=True)

    thin = [swap(s) for s in sends]
    thin = [
        t.reshape(groups, 2, capacity, width).transpose(1, 0, 2, 3).reshape(2, rows, width) for t in thin
    ]
    wide = [lax.all_gather(t, "dp", axis=2, tiled=True) for t in thin]
    math = [expert_math(x[0], x[1], *w) for x, w in zip(wide, weights)]
    summed = [lax.psum_scatter(m[3], "dp", scatter_dimension=2, tiled=True) for m in math]
    back = [
        s.reshape(2, groups, capacity, width).transpose(1, 0, 2, 3).reshape(groups * 2 * capacity, width)
        for s in summed
    ]
    got = [swap(b).reshape(groups * 2 * capacity, width) for b in back]
    carried = ()
    for part in range(local_copies):
        carried = combine(code, gate_t, cotangent, got[part], carried, part, part == owned, *sizes)
    layer_out, token_grad, gate_part = carried
    gate_grad = lax.all_to_all(
        gate_part.reshape(fanout, 1, tok_dev), "dp", split_axis=0, concat_axis=0, tiled=True
    ).sum(axis=0)

    def grads(pick, left):
        def one(i):
            return jnp.einsum("mf,md->fd", left(math[i]), pick(wide[i]), preferred_element_type=F32)

        extra = one(owned)
        return jnp.stack(
            [(one(i) + jnp.where(own_pick == i, 1.0, 0.0) * extra).astype(BF) for i in range(owned)]
        )

    w_gate_grad = grads(lambda x: x[0], lambda m: m[1])
    w_up_grad = grads(lambda x: x[0], lambda m: m[2])
    w_down_grad = grads(lambda x: x[1], lambda m: m[0])
    return (layer_out, token_grad, gate_grad.reshape(tok_dev, 1), w_gate_grad, w_up_grad, w_down_grad)


def solution(mesh):
    in_specs = (
        P("expert", "dp"),
        P("expert", "dp"),
        P("expert", None),
        P("expert", None),
        P(),
        P("expert", "dp", None),
        P("expert", "dp", None),
        P("expert", "dp", None),
    )
    out_specs = (
        P("expert", "dp"),
        P("expert", "dp"),
        P("expert", "dp"),
        P("expert", "dp", None),
        P("expert", "dp", None),
        P("expert", "dp", None),
    )
    return jax.shard_map(body, mesh=mesh, in_specs=in_specs, out_specs=out_specs, check_vma=False)
```

```python
import functools

import jax
import jax.numpy as jnp
from jax import lax
from jax.experimental import pallas as pl
from jax.experimental.pallas import tpu as pltpu
from jax.sharding import PartitionSpec as P

BF = jnp.bfloat16
F32 = jnp.float32


def row_codes(first, rows, tok_dev, part, groups, owned, capacity):
    local_copies = owned + 1
    r = first + lax.broadcasted_iota(jnp.int32, (rows, tok_dev), 0)
    wide = 2 * capacity
    group = (r.astype(F32) * (1.0 / wide) + 0.5 / wide).astype(jnp.int32)
    inside = r - group * wide
    front = inside < capacity
    place = jnp.where(front, inside, inside - capacity)
    if part < owned:
        copy = group * local_copies + part
    else:
        holder = group + groups // 2
        holder = jnp.where(holder >= groups, holder - groups, holder)
        copy = holder * local_copies + owned
    return copy * capacity + place, front


def send_kernel(owned, groups, capacity, block, route_ref, gate_ref, tok_ref, cot_ref, code_ref, *out_refs):
    fanout, tok_dev = route_ref.shape
    copies = groups * (owned + 1)
    ids = lax.broadcasted_iota(jnp.int32, (copies, tok_dev), 0)
    named = jnp.zeros((copies, tok_dev), F32)
    for k in range(fanout):
        named = jnp.where(route_ref[k : k + 1, :] == ids, 1.0, named)
    before = lax.broadcasted_iota(jnp.int32, (tok_dev, tok_dev), 0) < lax.broadcasted_iota(
        jnp.int32, (tok_dev, tok_dev), 1
    )
    rank = jnp.dot(named.astype(BF), jnp.where(before, 1.0, 0.0).astype(BF), preferred_element_type=F32)
    codes, gates = [], []
    for k in range(fanout):
        row = route_ref[k : k + 1, :]
        at = jnp.sum(jnp.where(row == ids, rank, 0.0), axis=0, keepdims=True)
        codes.append(row * capacity + at.astype(jnp.int32))
        gates.append(gate_ref[k : k + 1, :])
    code_ref[...] = jnp.concatenate(codes, axis=0)
    both = jnp.concatenate([tok_ref[...], cot_ref[...]], axis=0)
    for part, out_ref in enumerate(out_refs):
        for first in range(0, out_ref.shape[0], block):
            slot, front = row_codes(first, block, tok_dev, part, groups, owned, capacity)
            match = jnp.zeros((block, tok_dev), F32)
            scale = jnp.zeros((block, tok_dev), F32)
            for k in range(fanout):
                same = codes[k] == slot
                match = jnp.where(same, 1.0, match)
                scale = jnp.where(same, gates[k], scale)
            pick = jnp.concatenate([jnp.where(front, match, 0.0), jnp.where(front, 0.0, match)], axis=1)
            rows = jnp.dot(pick.astype(BF), both, preferred_element_type=F32)
            scale = jnp.sum(jnp.where(front, 0.0, scale), axis=1, keepdims=True)
            scale = jnp.where(front[:, :1], 1.0, scale)
            out_ref[first : first + block, :] = (rows * scale).astype(BF)


def send_rows(route_t, gate_t, tokens, cot, owned, groups, capacity):
    rows, width = groups * 2 * capacity, tokens.shape[1]
    out = pl.pallas_call(
        functools.partial(send_kernel, owned, groups, capacity, 4 * 2 * capacity),
        out_shape=[jax.ShapeDtypeStruct(route_t.shape, jnp.int32)]
        + [jax.ShapeDtypeStruct((rows, width), BF)] * (owned + 1),
        name="send_rows",
    )(route_t, gate_t, tokens, cot)
    return out[0], out[1:]


def combine_kernel(owned, groups, capacity, part, first_call, last_call, *refs):
    code_ref, gate_ref, cot_ref, got_ref = refs[:4]
    acc_ref, gp_ref = (None, None) if first_call else refs[4:6]
    outs = refs[4:] if first_call else refs[6:]
    fanout, tok_dev = code_ref.shape
    got = got_ref[...]
    nt = (((1,), (1,)), ((), ()))
    tn = (((0,), (0,)), ((), ()))
    z = lax.dot_general(got, cot_ref[...], nt, preferred_element_type=F32)
    slot, front = row_codes(0, got.shape[0], tok_dev, part, groups, owned, capacity)
    match = jnp.zeros(z.shape, F32)
    scale = jnp.zeros(z.shape, F32)
    zf = jnp.where(front, z, 0.0)
    parts = []
    for k in range(fanout):
        same = code_ref[k : k + 1, :] == slot
        match = jnp.where(same, 1.0, match)
        scale = jnp.where(same, gate_ref[k : k + 1, :], scale)
        parts.append(jnp.sum(jnp.where(same, zf, 0.0), axis=0, keepdims=True))
    scale = jnp.where(front, scale, 0.0)
    high = scale.astype(BF)
    low = (scale - high.astype(F32)).astype(BF)
    back = jnp.where(front, 0.0, match).astype(BF)
    weights = jnp.concatenate([high, low, back], axis=1)
    acc = lax.dot_general(weights, got, tn, preferred_element_type=F32)
    gp = jnp.concatenate(parts, axis=0)
    if not first_call:
        acc = acc + acc_ref[...]
        gp = gp + gp_ref[...]
    if last_call:
        outs[0][...] = (acc[:tok_dev] + acc[tok_dev : 2 * tok_dev]).astype(BF)
        outs[1][...] = acc[2 * tok_dev :].astype(BF)
        outs[2][...] = gp
    else:
        outs[0][...] = acc
        outs[1][...] = gp


def combine(code, gate_t, cot, got, carried, part, last_call, owned, groups, capacity):
    tok_dev, width = cot.shape
    gp_shape = jax.ShapeDtypeStruct(code.shape, F32)
    if last_call:
        out_shape = [jax.ShapeDtypeStruct((tok_dev, width), BF)] * 2 + [gp_shape]
    else:
        out_shape = [jax.ShapeDtypeStruct((3 * tok_dev, width), F32), gp_shape]
    return pl.pallas_call(
        functools.partial(combine_kernel, owned, groups, capacity, part, not carried, last_call),
        out_shape=out_shape,
        name=f"combine_{part}",
    )(code, gate_t, cot, got, *carried)


def dot_nt(x, w):
    return lax.dot_general(x, w, (((1,), (1,)), ((), ())), preferred_element_type=F32)


def dot_nn(x, w):
    return jnp.dot(x, w, preferred_element_type=F32)


def math_kernel(width, at_ref, *refs):
    own, right, left, opp_in, opp_cot, p_own, p_right, p_left, p_opp_in, p_opp_cot = refs[:10]
    gate_ref, up_ref, down_ref, all_ref, acts_ref = refs[10:15]
    outs = refs[15:]
    for q, piece in ((0, own), (1, right), (2, left), (4, p_own), (5, p_right), (6, p_left)):
        all_ref[:, :, pl.ds(pl.multiple_of(at_ref[q], width), width)] = piece[...]
    for q, halves in ((3, (opp_in, opp_cot)), (7, (p_opp_in, p_opp_cot))):
        for h in range(2):
            all_ref[h, :, pl.ds(pl.multiple_of(at_ref[q], width), width)] = halves[h][...]
    gate_act = dot_nt(all_ref[0], gate_ref[0])
    up_act = dot_nt(all_ref[0], up_ref[0])
    d_hidden = dot_nt(all_ref[1], down_ref[0])
    s = jax.nn.sigmoid(gate_act)
    activated = gate_act * s
    hidden = activated * up_act
    d_gate = d_hidden * up_act * s * (1.0 + gate_act * (1.0 - s))
    d_up = d_hidden * activated
    for n, act in enumerate((hidden, d_gate, d_up)):
        acts_ref[n] = act.T.astype(BF)
    hidden, d_gate, d_up = hidden.astype(BF), d_gate.astype(BF), d_up.astype(BF)
    for q, (ref, n) in enumerate(
        ((outs[0], 0), (outs[0], 1), (outs[0], 2), (outs[1], None), (outs[2], 0), (outs[2], 1), (outs[2], 2), (outs[3], None))
    ):
        at = pl.ds(pl.multiple_of(at_ref[q], width), width)
        out = dot_nn(hidden, down_ref[0, :, at]).astype(BF)
        back = (dot_nn(d_gate, gate_ref[0, :, at]) + dot_nn(d_up, up_ref[0, :, at])).astype(BF)
        where = () if n is None else (n,)
        ref[(*where, 0)] = out
        ref[(*where, 1)] = back


def expert_math(at, pieces, weights, part, owned):
    rows, width = pieces[3].shape
    features = weights[0].shape[2]
    hidden = weights[0].shape[1]

    def whole(shape):
        return pl.BlockSpec(shape, lambda i, at: (0,) * len(shape))

    if part < owned:
        w_spec = pl.BlockSpec((1, hidden, features), lambda i, at: (part, 0, 0))
    else:
        w_spec = pl.BlockSpec((1, hidden, features), lambda i, at: (at[8], 0, 0))
    out_shape = [
        jax.ShapeDtypeStruct(shape, BF)
        for shape in (
            (2, rows, features),
            (3, hidden, rows),
            (3, 2, rows, width),
            (2, rows, width),
            (3, 2, rows, width),
            (2, rows, width),
        )
    ]
    return pl.pallas_call(
        functools.partial(math_kernel, width),
        grid_spec=pltpu.PrefetchScalarGridSpec(
            num_scalar_prefetch=1,
            grid=(1,),
            in_specs=[whole(p.shape) for p in pieces] + [w_spec] * 3,
            out_specs=[whole(o.shape) for o in out_shape],
        ),
        out_shape=out_shape,
        compiler_params=pltpu.CompilerParams(vmem_limit_bytes=56 * 1024 * 1024),
        name=f"expert_math_{part}",
    )(at, *pieces, *weights)


def grads_kernel(owned, pick_ref, *refs):
    wide, acts, outs = refs[: owned + 1], refs[owned + 1 : 2 * owned + 2], refs[2 * owned + 2 :]
    for out_ref, n, which in zip(outs, (1, 2, 0), (0, 0, 1)):
        extra = dot_nn(acts[owned][n], wide[owned][which])
        for i in range(owned):
            keep = jnp.where(pick_ref[0] == i, 1.0, 0.0)
            out_ref[i] = (dot_nn(acts[i][n], wide[i][which]) + keep * extra).astype(BF)


def grads(pick, wide, acts, owned):
    _, rows, features = wide[0].shape
    hidden = acts[0].shape[1]
    block = features // 4
    return pl.pallas_call(
        functools.partial(grads_kernel, owned),
        grid_spec=pltpu.PrefetchScalarGridSpec(
            num_scalar_prefetch=1,
            grid=(features // block,),
            in_specs=[pl.BlockSpec((2, rows, block), lambda i, p: (0, 0, i))] * (owned + 1)
            + [pl.BlockSpec((3, hidden, rows), lambda i, p: (0, 0, 0))] * (owned + 1),
            out_specs=[pl.BlockSpec((owned, hidden, block), lambda i, p: (0, 0, i))] * 3,
        ),
        out_shape=[jax.ShapeDtypeStruct((owned, hidden, features), BF)] * 3,
        compiler_params=pltpu.CompilerParams(vmem_limit_bytes=56 * 1024 * 1024),
        name="weight_grads",
    )(pick, *wide, *acts)


def hop(x, by):
    n = lax.axis_size("dp")
    return lax.ppermute(x, "dp", [(i, (i + 2 * by) % n) for i in range(n)])


def twin(x):
    return lax.ppermute(x, "dp", [(i, i ^ 1) for i in range(lax.axis_size("dp"))])


def spread(own):
    left, right = hop(own, 1), hop(own, -1)
    opp_in, opp_cot = hop(left[0], 1), hop(right[1], -1)
    mine = (own, right, left, opp_in, opp_cot)
    return (*mine, *(twin(piece) for piece in mine))


def gathered_sum(near, near_opp, far, far_opp):
    both_opp = (near_opp.astype(F32) + twin(far_opp).astype(F32)).astype(BF)
    both = near.astype(F32) + twin(far).astype(F32)
    from_left, from_right = hop(both_opp[0], 1).astype(F32), hop(both_opp[1], -1).astype(F32)
    to_right = jnp.stack([both[1, 0] + from_left, both[1, 1]]).astype(BF)
    to_left = jnp.stack([both[2, 0], both[2, 1] + from_right]).astype(BF)
    return (both[0] + hop(to_right, 1).astype(F32) + hop(to_left, -1).astype(F32)).astype(BF)


def body(tokens, cotangent, route, gate_prob, replica_pick, w_gate, w_up, w_down):
    groups = lax.axis_size("expert")
    column = lax.axis_index("expert")
    tok_dev, width = tokens.shape
    fanout = route.shape[1]
    owned = w_gate.shape[0]
    local_copies = owned + 1
    capacity = tok_dev * fanout // (groups * local_copies) + 2
    sizes = (owned, groups, capacity)
    rows = groups * capacity
    route_t, gate_t = route.T, gate_prob.T
    code, sends = send_rows(route_t, gate_t, tokens, cotangent, *sizes)

    own_pick = replica_pick[(column + groups // 2) % groups]
    place = lax.axis_index("dp")
    steps = jnp.array([0, 1, 3, 2, 0, 1, 3, 2, 0], jnp.int32)
    flip = jnp.array([0, 0, 0, 0, 1, 1, 1, 1, 0], jnp.int32)
    at = 2 * ((place // 2 + steps) % 4) + (place % 2 + flip) % 2
    at = jnp.where(jnp.arange(9) == 8, own_pick, at * width).astype(jnp.int32)

    def swap(x):
        return lax.all_to_all(x.reshape(groups, 2 * capacity, width), "expert", split_axis=0, concat_axis=0, tiled=True)

    thin = [swap(s) for s in sends]
    thin = [
        t.reshape(groups, 2, capacity, width).transpose(1, 0, 2, 3).reshape(2, rows, width) for t in thin
    ]
    math = [
        expert_math(at, spread(t), (w_gate, w_up, w_down), part, owned) for part, t in enumerate(thin)
    ]
    summed = [gathered_sum(*m[2:]) for m in math]
    back = [
        s.reshape(2, groups, capacity, width).transpose(1, 0, 2, 3).reshape(groups * 2 * capacity, width)
        for s in summed
    ]
    got = [swap(b).reshape(groups * 2 * capacity, width) for b in back]
    carried = ()
    for part in range(local_copies):
        carried = combine(code, gate_t, cotangent, got[part], carried, part, part == owned, *sizes)
    layer_out, token_grad, gate_part = carried
    gate_grad = lax.all_to_all(
        gate_part.reshape(fanout, 1, tok_dev), "dp", split_axis=0, concat_axis=0, tiled=True
    ).sum(axis=0)

    w_gate_grad, w_up_grad, w_down_grad = grads(
        own_pick.reshape(1), [m[0] for m in math], [m[1] for m in math], owned
    )
    return (layer_out, token_grad, gate_grad.reshape(tok_dev, 1), w_gate_grad, w_up_grad, w_down_grad)


def solution(mesh):
    in_specs = (
        P("expert", "dp"),
        P("expert", "dp"),
        P("expert", None),
        P("expert", None),
        P(),
        P("expert", "dp", None),
        P("expert", "dp", None),
        P("expert", "dp", None),
    )
    out_specs = (
        P("expert", "dp"),
        P("expert", "dp"),
        P("expert", "dp"),
        P("expert", "dp", None),
        P("expert", "dp", None),
        P("expert", "dp", None),
    )
    return jax.shard_map(body, mesh=mesh, in_specs=in_specs, out_specs=out_specs, check_vma=False)
```

```python
import functools

import jax
import jax.numpy as jnp
from jax import lax
from jax.experimental import pallas as pl
from jax.experimental.pallas import tpu as pltpu
from jax.sharding import PartitionSpec as P


BF = jnp.bfloat16
F32 = jnp.float32


def row_codes(first, rows, tok_dev, part, groups, owned, capacity):
    local_copies = owned + 1
    r = first + lax.broadcasted_iota(jnp.int32, (rows, tok_dev), 0)
    wide = 2 * capacity
    group = (r.astype(F32) * (1.0 / wide) + 0.5 / wide).astype(jnp.int32)
    inside = r - group * wide
    front = inside < capacity
    place = jnp.where(front, inside, inside - capacity)
    if part < owned:
        copy = group * local_copies + part
    else:
        holder = group + groups // 2
        holder = jnp.where(holder >= groups, holder - groups, holder)
        copy = holder * local_copies + owned
    return copy * capacity + place, front


def send_kernel(owned, groups, capacity, block, route_ref, gate_ref, tok_ref, cot_ref, code_ref, *out_refs):
    fanout, tok_dev = route_ref.shape
    copies = groups * (owned + 1)
    ids = lax.broadcasted_iota(jnp.int32, (copies, tok_dev), 0)
    named = jnp.zeros((copies, tok_dev), F32)
    for k in range(fanout):
        named = jnp.where(route_ref[k : k + 1, :] == ids, 1.0, named)
    before = lax.broadcasted_iota(jnp.int32, (tok_dev, tok_dev), 0) < lax.broadcasted_iota(
        jnp.int32, (tok_dev, tok_dev), 1
    )
    rank = jnp.dot(named.astype(BF), jnp.where(before, 1.0, 0.0).astype(BF), preferred_element_type=F32)
    codes, gates = [], []
    for k in range(fanout):
        row = route_ref[k : k + 1, :]
        at = jnp.sum(jnp.where(row == ids, rank, 0.0), axis=0, keepdims=True)
        codes.append(row * capacity + at.astype(jnp.int32))
        gates.append(gate_ref[k : k + 1, :])
    code_ref[...] = jnp.concatenate(codes, axis=0)
    both = jnp.concatenate([tok_ref[...], cot_ref[...]], axis=0)
    for part, out_ref in enumerate(out_refs):
        @pl.loop(0, out_ref.shape[0] // block)
        def _(i, part=part, out_ref=out_ref):
            first = pl.multiple_of(i * block, block)
            slot, front = row_codes(first, block, tok_dev, part, groups, owned, capacity)
            match = jnp.zeros((block, tok_dev), F32)
            scale = jnp.zeros((block, tok_dev), F32)
            for k in range(fanout):
                same = codes[k] == slot
                match = jnp.where(same, 1.0, match)
                scale = jnp.where(same, gates[k], scale)
            pick = jnp.concatenate([jnp.where(front, match, 0.0), jnp.where(front, 0.0, match)], axis=1)
            rows = jnp.dot(pick.astype(BF), both, preferred_element_type=F32)
            scale = jnp.sum(jnp.where(front, 0.0, scale), axis=1, keepdims=True)
            scale = jnp.where(front[:, :1], 1.0, scale)
            out_ref[pl.ds(first, block), :] = (rows * scale).astype(BF)


def send_rows(route_t, gate_t, tokens, cot, owned, groups, capacity):
    rows, width = groups * 2 * capacity, tokens.shape[1]
    out = pl.pallas_call(
        functools.partial(send_kernel, owned, groups, capacity, 4 * 2 * capacity),
        out_shape=[jax.ShapeDtypeStruct(route_t.shape, jnp.int32)]
        + [jax.ShapeDtypeStruct((rows, width), BF)] * (owned + 1),
        name="send_rows",
    )(route_t, gate_t, tokens, cot)
    return out[0], out[1:]


def combine_kernel(owned, groups, capacity, part, first_call, last_call, *refs):
    code_ref, gate_ref, cot_ref, got_ref = refs[:4]
    acc_ref, gp_ref = (None, None) if first_call else refs[4:6]
    outs = refs[4:] if first_call else refs[6:]
    fanout, tok_dev = code_ref.shape
    nt = (((1,), (1,)), ((), ()))
    tn = (((0,), (0,)), ((), ()))
    block = 8 * 2 * capacity

    def step(i, carried):
        acc, gp = carried
        first = pl.multiple_of(i * block, block)
        got = got_ref[pl.ds(first, block), :]
        z = lax.dot_general(got, cot_ref[...], nt, preferred_element_type=F32)
        slot, front = row_codes(first, block, tok_dev, part, groups, owned, capacity)
        match = jnp.zeros(z.shape, F32)
        scale = jnp.zeros(z.shape, F32)
        zf = jnp.where(front, z, 0.0)
        parts = []
        for k in range(fanout):
            same = code_ref[k : k + 1, :] == slot
            match = jnp.where(same, 1.0, match)
            scale = jnp.where(same, gate_ref[k : k + 1, :], scale)
            parts.append(jnp.sum(jnp.where(same, zf, 0.0), axis=0, keepdims=True))
        scale = jnp.where(front, scale, 0.0)
        high = scale.astype(BF)
        low = (scale - high.astype(F32)).astype(BF)
        back = jnp.where(front, 0.0, match).astype(BF)
        weights = jnp.concatenate([high, low, back], axis=1)
        acc = acc + lax.dot_general(weights, got, tn, preferred_element_type=F32)
        return acc, gp + jnp.concatenate(parts, axis=0)

    start = (jnp.zeros((3 * tok_dev, cot_ref.shape[1]), F32), jnp.zeros((fanout, tok_dev), F32))
    acc, gp = lax.fori_loop(0, got_ref.shape[0] // block, step, start)
    if not first_call:
        acc = acc + acc_ref[...]
        gp = gp + gp_ref[...]
    if last_call:
        outs[0][...] = (acc[:tok_dev] + acc[tok_dev : 2 * tok_dev]).astype(BF)
        outs[1][...] = acc[2 * tok_dev :].astype(BF)
        outs[2][...] = gp
    else:
        outs[0][...] = acc
        outs[1][...] = gp


def combine(code, gate_t, cot, got, carried, part, last_call, owned, groups, capacity):
    tok_dev, width = cot.shape
    gp_shape = jax.ShapeDtypeStruct(code.shape, F32)
    if last_call:
        out_shape = [jax.ShapeDtypeStruct((tok_dev, width), BF)] * 2 + [gp_shape]
    else:
        out_shape = [jax.ShapeDtypeStruct((3 * tok_dev, width), F32), gp_shape]
    return pl.pallas_call(
        functools.partial(combine_kernel, owned, groups, capacity, part, not carried, last_call), out_shape=out_shape
    )(code, gate_t, cot, got, *carried)


def dot_nt(x, w):
    return lax.dot_general(x, w, (((1,), (1,)), ((), ())), preferred_element_type=F32)


def dot_nn(x, w):
    return jnp.dot(x, w, preferred_element_type=F32)


def math_kernel(width, at_ref, *refs):
    own, right, left, opp_in, opp_cot, p_own, p_right, p_left, p_opp_in, p_opp_cot = refs[:10]
    gate_ref, up_ref, down_ref, all_ref, acts_ref = refs[10:15]
    outs = refs[15:]
    for q, piece in ((0, own), (1, right), (2, left), (4, p_own), (5, p_right), (6, p_left)):
        all_ref[:, :, pl.ds(pl.multiple_of(at_ref[q], width), width)] = piece[...]
    for q, halves in ((3, (opp_in, opp_cot)), (7, (p_opp_in, p_opp_cot))):
        for h in range(2):
            all_ref[h, :, pl.ds(pl.multiple_of(at_ref[q], width), width)] = halves[h][...]
    gate_act = dot_nt(all_ref[0], gate_ref[0])
    up_act = dot_nt(all_ref[0], up_ref[0])
    d_hidden = dot_nt(all_ref[1], down_ref[0])
    s = jax.nn.sigmoid(gate_act)
    activated = gate_act * s
    hidden = activated * up_act
    d_gate = d_hidden * up_act * s * (1.0 + gate_act * (1.0 - s))
    d_up = d_hidden * activated
    for n, act in enumerate((hidden, d_gate, d_up)):
        acts_ref[n] = act.T.astype(BF)
    hidden, d_gate, d_up = hidden.astype(BF), d_gate.astype(BF), d_up.astype(BF)
    for q, (ref, n) in enumerate(
        ((outs[0], 0), (outs[0], 1), (outs[0], 2), (outs[1], None), (outs[2], 0), (outs[2], 1), (outs[2], 2), (outs[3], None))
    ):
        at = pl.ds(pl.multiple_of(at_ref[q], width), width)
        out = dot_nn(hidden, down_ref[0, :, at]).astype(BF)
        back = (dot_nn(d_gate, gate_ref[0, :, at]) + dot_nn(d_up, up_ref[0, :, at])).astype(BF)
        where = () if n is None else (n,)
        ref[(*where, 0)] = out
        ref[(*where, 1)] = back


def expert_math(at, pieces, weights, part, owned):
    rows, width = pieces[3].shape
    features = weights[0].shape[2]
    hidden = weights[0].shape[1]

    def whole(shape):
        return pl.BlockSpec(shape, lambda i, at: (0,) * len(shape))

    if part < owned:
        w_spec = pl.BlockSpec((1, hidden, features), lambda i, at: (part, 0, 0))
    else:
        w_spec = pl.BlockSpec((1, hidden, features), lambda i, at: (at[8], 0, 0))
    out_shape = [
        jax.ShapeDtypeStruct(shape, BF)
        for shape in (
            (2, rows, features),
            (3, hidden, rows),
            (3, 2, rows, width),
            (2, rows, width),
            (3, 2, rows, width),
            (2, rows, width),
        )
    ]
    return pl.pallas_call(
        functools.partial(math_kernel, width),
        grid_spec=pltpu.PrefetchScalarGridSpec(
            num_scalar_prefetch=1,
            grid=(1,),
            in_specs=[whole(p.shape) for p in pieces] + [w_spec] * 3,
            out_specs=[whole(o.shape) for o in out_shape],
        ),
        out_shape=out_shape,
        compiler_params=pltpu.CompilerParams(vmem_limit_bytes=56 * 1024 * 1024),
    )(at, *pieces, *weights)


def grads_kernel(owned, pick_ref, *refs):
    wide, acts, outs = refs[: owned + 1], refs[owned + 1 : 2 * owned + 2], refs[2 * owned + 2 :]
    for out_ref, n, which in zip(outs, (1, 2, 0), (0, 0, 1)):
        extra = dot_nn(acts[owned][n], wide[owned][which])
        for i in range(owned):
            keep = jnp.where(pick_ref[0] == i, 1.0, 0.0)
            out_ref[i] = (dot_nn(acts[i][n], wide[i][which]) + keep * extra).astype(BF)


def grads(pick, wide, acts, owned):
    _, rows, features = wide[0].shape
    hidden = acts[0].shape[1]
    block = features // 4
    return pl.pallas_call(
        functools.partial(grads_kernel, owned),
        grid_spec=pltpu.PrefetchScalarGridSpec(
            num_scalar_prefetch=1,
            grid=(features // block,),
            in_specs=[pl.BlockSpec((2, rows, block), lambda i, p: (0, 0, i))] * (owned + 1)
            + [pl.BlockSpec((3, hidden, rows), lambda i, p: (0, 0, 0))] * (owned + 1),
            out_specs=[pl.BlockSpec((owned, hidden, block), lambda i, p: (0, 0, i))] * 3,
        ),
        out_shape=[jax.ShapeDtypeStruct((owned, hidden, features), BF)] * 3,
        compiler_params=pltpu.CompilerParams(vmem_limit_bytes=56 * 1024 * 1024),
        name="weight_grads",
    )(pick, *wide, *acts)


def hop(x, by):
    n = lax.axis_size("dp")
    return lax.ppermute(x, "dp", [(i, (i + 2 * by) % n) for i in range(n)])


def twin(x):
    return lax.ppermute(x, "dp", [(i, i ^ 1) for i in range(lax.axis_size("dp"))])


def spread(own):
    left, right = hop(own, 1), hop(own, -1)
    opp_in, opp_cot = hop(left[0], 1), hop(right[1], -1)
    mine = (own, right, left, opp_in, opp_cot)
    return (*mine, *(twin(piece) for piece in mine))


def gathered_sum(near, near_opp, far, far_opp):
    both_opp = (near_opp.astype(F32) + twin(far_opp).astype(F32)).astype(BF)
    both = near.astype(F32) + twin(far).astype(F32)
    from_left = hop(both_opp[0], 1).astype(F32)
    from_right = hop(both_opp[1], -1).astype(F32)
    to_right = jnp.stack([both[1, 0] + from_left, both[1, 1]]).astype(BF)
    to_left = jnp.stack([both[2, 0], both[2, 1] + from_right]).astype(BF)
    to_left, to_right = hop(to_left, -1), hop(to_right, 1)
    return (both[0] + to_right.astype(F32) + to_left.astype(F32)).astype(BF)


def body(tokens, cotangent, route, gate_prob, replica_pick, w_gate, w_up, w_down):
    groups = lax.axis_size("expert")
    column = lax.axis_index("expert")
    tok_dev, width = tokens.shape
    fanout = route.shape[1]
    owned = w_gate.shape[0]
    local_copies = owned + 1
    capacity = tok_dev * fanout // (groups * local_copies) + 2
    sizes = (owned, groups, capacity)
    rows = groups * capacity
    route_t, gate_t = route.T, gate_prob.T
    code, sends = send_rows(route_t, gate_t, tokens, cotangent, *sizes)

    own_pick = replica_pick[(column + groups // 2) % groups]
    place = lax.axis_index("dp")
    steps = jnp.array([0, 1, 3, 2, 0, 1, 3, 2, 0], jnp.int32)
    flip = jnp.array([0, 0, 0, 0, 1, 1, 1, 1, 0], jnp.int32)
    at = 2 * ((place // 2 + steps) % 4) + (place % 2 + flip) % 2
    at = jnp.where(jnp.arange(9) == 8, own_pick, at * width).astype(jnp.int32)

    def swap(x):
        return lax.all_to_all(x.reshape(groups, 2 * capacity, width), "expert", split_axis=0, concat_axis=0, tiled=True)

    got, math = [], []
    for part, send in enumerate(sends):
        thin = swap(send)
        thin = thin.reshape(groups, 2, capacity, width).transpose(1, 0, 2, 3).reshape(2, rows, width)
        pieces = spread(thin)
        math.append(expert_math(at, pieces, (w_gate, w_up, w_down), part, owned))
        back = gathered_sum(*math[-1][2:])
        back = back.reshape(2, groups, capacity, width).transpose(1, 0, 2, 3)
        got.append(swap(back).reshape(groups * 2 * capacity, width))
    carried = ()
    for part in range(local_copies):
        carried = combine(code, gate_t, cotangent, got[part], carried, part, part == owned, *sizes)
    layer_out, token_grad, gate_part = carried
    n = lax.axis_size("dp")
    gate_grad = lax.dynamic_index_in_dim(gate_part, place, 0, keepdims=False)
    for by in range(1, n):
        gone = lax.dynamic_index_in_dim(gate_part, (place + by) % n, 0, keepdims=False)
        gate_grad = gate_grad + lax.ppermute(gone, "dp", [(i, (i + by) % n) for i in range(n)])

    w_gate_grad, w_up_grad, w_down_grad = grads(own_pick.reshape(1), [m[0] for m in math], [m[1] for m in math], owned)
    return (layer_out, token_grad, gate_grad.reshape(tok_dev, 1), w_gate_grad, w_up_grad, w_down_grad)


def solution(mesh):
    in_specs = (
        P("expert", "dp"),
        P("expert", "dp"),
        P("expert", None),
        P("expert", None),
        P(),
        P("expert", "dp", None),
        P("expert", "dp", None),
        P("expert", "dp", None),
    )
    out_specs = (
        P("expert", "dp"),
        P("expert", "dp"),
        P("expert", "dp"),
        P("expert", "dp", None),
        P("expert", "dp", None),
        P("expert", "dp", None),
    )

    return jax.shard_map(body, mesh=mesh, in_specs=in_specs, out_specs=out_specs, check_vma=False)
```

```python
import functools

import jax
import jax.numpy as jnp
from jax import lax
from jax.experimental import pallas as pl
from jax.experimental.pallas import tpu as pltpu
from jax.sharding import PartitionSpec as P


BF = jnp.bfloat16
F32 = jnp.float32


def row_codes(first, shape, axis, part, groups, owned, capacity):
    local_copies = owned + 1
    r = first + lax.broadcasted_iota(jnp.int32, shape, axis)
    wide = 2 * capacity
    group = (r.astype(F32) * (1.0 / wide) + 0.5 / wide).astype(jnp.int32)
    inside = r - group * wide
    front = inside < capacity
    place = jnp.where(front, inside, inside - capacity)
    if part < owned:
        copy = group * local_copies + part
    else:
        holder = group + groups // 2
        holder = jnp.where(holder >= groups, holder - groups, holder)
        copy = holder * local_copies + owned
    return copy * capacity + place, front


def send_kernel(owned, groups, capacity, block, route_ref, gate_ref, tok_ref, cot_ref, code_ref, *out_refs):
    fanout, tok_dev = route_ref.shape
    copies = groups * (owned + 1)
    ids = lax.broadcasted_iota(jnp.int32, (copies, tok_dev), 0)
    named = jnp.zeros((copies, tok_dev), F32)
    for k in range(fanout):
        named = jnp.where(route_ref[k : k + 1, :] == ids, 1.0, named)
    before = lax.broadcasted_iota(jnp.int32, (tok_dev, tok_dev), 0) < lax.broadcasted_iota(
        jnp.int32, (tok_dev, tok_dev), 1
    )
    rank = jnp.dot(named.astype(BF), jnp.where(before, 1.0, 0.0).astype(BF), preferred_element_type=F32)
    codes, gates = [], []
    for k in range(fanout):
        row = route_ref[k : k + 1, :]
        at = jnp.sum(jnp.where(row == ids, rank, 0.0), axis=0, keepdims=True)
        codes.append(row * capacity + at.astype(jnp.int32))
        gates.append(gate_ref[k : k + 1, :])
    code_ref[...] = jnp.concatenate(codes, axis=0)
    both = jnp.concatenate([tok_ref[...], cot_ref[...]], axis=0)
    for part, out_ref in enumerate(out_refs):
        for first in range(0, out_ref.shape[0], block):
            slot, front = row_codes(first, (block, tok_dev), 0, part, groups, owned, capacity)
            match = jnp.zeros((block, tok_dev), F32)
            scale = jnp.zeros((block, tok_dev), F32)
            for k in range(fanout):
                same = codes[k] == slot
                match = jnp.where(same, 1.0, match)
                scale = jnp.where(same, gates[k], scale)
            pick = jnp.concatenate([jnp.where(front, match, 0.0), jnp.where(front, 0.0, match)], axis=1)
            rows = jnp.dot(pick.astype(BF), both, preferred_element_type=F32)
            scale = jnp.sum(jnp.where(front, 0.0, scale), axis=1, keepdims=True)
            scale = jnp.where(front[:, :1], 1.0, scale)
            out_ref[first : first + block, :] = (rows * scale).astype(BF)


def send_rows(route_t, gate_t, tokens, cot, owned, groups, capacity):
    rows, width = groups * 2 * capacity, tokens.shape[1]
    out = pl.pallas_call(
        functools.partial(send_kernel, owned, groups, capacity, 4 * 2 * capacity),
        out_shape=[jax.ShapeDtypeStruct(route_t.shape, jnp.int32)]
        + [jax.ShapeDtypeStruct((rows, width), BF)] * (owned + 1),
        name="send_rows",
    )(route_t, gate_t, tokens, cot)
    return out[0], out[1:]


def weights_kernel(owned, groups, capacity, code_ref, gate_ref, out_ref):
    tok_dev, fanout = code_ref.shape
    lanes = 128
    for part in range(owned + 1):
        @pl.loop(0, out_ref.shape[2] // lanes)
        def _(i, part=part):
            first = pl.multiple_of(i * lanes, lanes)
            slot, front = row_codes(first, (tok_dev, lanes), 1, part, groups, owned, capacity)
            match = jnp.zeros((tok_dev, lanes), F32)
            scale = jnp.zeros((tok_dev, lanes), F32)
            for k in range(fanout):
                same = code_ref[:, k : k + 1] == slot
                match = jnp.where(same, 1.0, match)
                scale = jnp.where(same, gate_ref[:, k : k + 1], scale)
            scale = jnp.where(front, scale, 0.0)
            high = scale.astype(BF)
            out_ref[part, :tok_dev, pl.ds(first, lanes)] = high
            out_ref[part, tok_dev : 2 * tok_dev, pl.ds(first, lanes)] = (scale - high.astype(F32)).astype(BF)
            out_ref[part, 2 * tok_dev :, pl.ds(first, lanes)] = jnp.where(front, 0.0, match).astype(BF)


def combine_weights(code, gate, owned, groups, capacity):
    tok_dev = code.shape[0]
    return pl.pallas_call(
        functools.partial(weights_kernel, owned, groups, capacity),
        out_shape=jax.ShapeDtypeStruct((owned + 1, 3 * tok_dev, groups * 2 * capacity), BF),
        name="combine_weights",
    )(code, gate)


def dot_nt(x, w):
    return lax.dot_general(x, w, (((1,), (1,)), ((), ())), preferred_element_type=F32)


def dot_nn(x, w):
    return jnp.dot(x, w, preferred_element_type=F32)


def math_kernel(width, at_ref, *refs):
    own, right, left, opp_in, opp_cot, p_own, p_side, p_opp = refs[:8]
    gate_ref, up_ref, down_ref, all_ref, acts_ref, sums_ref = refs[8:14]
    outs = refs[14:]

    def place(q):
        return pl.ds(pl.multiple_of(at_ref[q], width), width)

    for q, piece in enumerate((own[...], right[...], left[...], None, p_own[...], p_side[0], p_side[1], p_opp[...])):
        if piece is not None:
            all_ref[:, :, place(q)] = piece
    all_ref[0, :, place(3)] = opp_in[...]
    all_ref[1, :, place(3)] = opp_cot[...]
    gate_act = dot_nt(all_ref[0], gate_ref[0])
    up_act = dot_nt(all_ref[0], up_ref[0])
    d_hidden = dot_nt(all_ref[1], down_ref[0])
    s = jax.nn.sigmoid(gate_act)
    activated = gate_act * s
    hidden = (activated * up_act).astype(BF)
    d_gate = d_hidden * up_act * s * (1.0 + gate_act * (1.0 - s))
    d_up = d_hidden * activated
    sums_ref[...] = jnp.sum((hidden.astype(F32) * d_hidden).T, axis=0, keepdims=True)
    for n, act in enumerate((hidden.astype(F32), d_gate, d_up)):
        acts_ref[n] = act.T.astype(BF)
    d_gate, d_up = d_gate.astype(BF), d_up.astype(BF)
    for q in range(8):
        at = place(q)
        out = dot_nn(hidden, down_ref[0, :, at]).astype(BF)
        back = (dot_nn(d_gate, gate_ref[0, :, at]) + dot_nn(d_up, up_ref[0, :, at])).astype(BF)
        ref, where = outs[2 * (q // 4) + (q % 4) // 3], (() if q % 4 == 3 else (q % 4,))
        ref[(*where, 0)] = out
        ref[(*where, 1)] = back


def expert_math(at, pieces, weights, part, owned):
    rows, width = pieces[3].shape
    hidden, features = weights[0].shape[1:]
    block = 128

    def rowwise(shape, axis):
        cut = tuple(block if n == axis else d for n, d in enumerate(shape))
        return pl.BlockSpec(cut, lambda i, at: tuple(i if n == axis else 0 for n in range(len(shape))))

    if part < owned:
        w_spec = pl.BlockSpec((1, hidden, features), lambda i, at: (part, 0, 0))
    else:
        w_spec = pl.BlockSpec((1, hidden, features), lambda i, at: (at[8], 0, 0))
    outs = (
        ((2, rows, features), BF, 1),
        ((3, hidden, rows), BF, 2),
        ((1, rows), F32, 1),
        ((3, 2, rows, width), BF, 2),
        ((2, rows, width), BF, 1),
        ((3, 2, rows, width), BF, 2),
        ((2, rows, width), BF, 1),
    )
    return pl.pallas_call(
        functools.partial(math_kernel, width),
        grid_spec=pltpu.PrefetchScalarGridSpec(
            num_scalar_prefetch=1,
            grid=(rows // block,),
            in_specs=[rowwise(p.shape, p.ndim - 2) for p in pieces] + [w_spec] * 3,
            out_specs=[rowwise(shape, axis) for shape, _, axis in outs],
        ),
        out_shape=[jax.ShapeDtypeStruct(shape, kind) for shape, kind, _ in outs],
        compiler_params=pltpu.CompilerParams(vmem_limit_bytes=56 * 1024 * 1024),
    )(at, *pieces, *weights)


def grads_kernel(owned, pick_ref, *refs):
    wide, acts, outs = refs[: owned + 1], refs[owned + 1 : 2 * owned + 2], refs[2 * owned + 2 :]
    for out_ref, n, which in zip(outs, (1, 2, 0), (0, 0, 1)):
        extra = dot_nn(acts[owned][n], wide[owned][which])
        for i in range(owned):
            keep = jnp.where(pick_ref[0] == i, 1.0, 0.0)
            out_ref[i] = (dot_nn(acts[i][n], wide[i][which]) + keep * extra).astype(BF)


def grads(pick, wide, acts, owned):
    _, rows, features = wide[0].shape
    hidden = acts[0].shape[1]
    block = features // 4
    return pl.pallas_call(
        functools.partial(grads_kernel, owned),
        grid_spec=pltpu.PrefetchScalarGridSpec(
            num_scalar_prefetch=1,
            grid=(features // block,),
            in_specs=[pl.BlockSpec((2, rows, block), lambda i, p: (0, 0, i))] * (owned + 1)
            + [pl.BlockSpec((3, hidden, rows), lambda i, p: (0, 0, 0))] * (owned + 1),
            out_specs=[pl.BlockSpec((owned, hidden, block), lambda i, p: (0, 0, i))] * 3,
        ),
        out_shape=[jax.ShapeDtypeStruct((owned, hidden, features), BF)] * 3,
        compiler_params=pltpu.CompilerParams(vmem_limit_bytes=56 * 1024 * 1024),
        name="weight_grads",
    )(pick, *wide, *acts)


def hop(x, by):
    n = lax.axis_size("dp")
    return lax.ppermute(x, "dp", [(i, (i + 2 * by) % n) for i in range(n)])


def twin(x):
    return lax.ppermute(x, "dp", [(i, i ^ 1) for i in range(lax.axis_size("dp"))])


def spread(own):
    left, right = hop(own, 1), hop(own, -1)
    opp_in, opp_cot = hop(left[0], 1), hop(right[1], -1)
    theirs = (own, jnp.stack([right, left]), jnp.stack([opp_in, opp_cot]))
    return (own, right, left, opp_in, opp_cot, *(twin(piece) for piece in theirs))


def gathered_sum(near, near_opp, far, far_opp):
    both_opp = (near_opp.astype(F32) + twin(far_opp).astype(F32)).astype(BF)
    both = near.astype(F32) + twin(far).astype(F32)
    from_left = hop(both_opp[0], 1).astype(F32)
    from_right = hop(both_opp[1], -1).astype(F32)
    to_right = jnp.stack([both[1, 0] + from_left, both[1, 1]]).astype(BF)
    to_left = jnp.stack([both[2, 0], both[2, 1] + from_right]).astype(BF)
    to_left, to_right = hop(to_left, -1), hop(to_right, 1)
    return (both[0] + to_right.astype(F32) + to_left.astype(F32)).astype(BF)


def body(tokens, cotangent, route, gate_prob, replica_pick, w_gate, w_up, w_down):
    groups = lax.axis_size("expert")
    column = lax.axis_index("expert")
    tok_dev, width = tokens.shape
    fanout = route.shape[1]
    owned = w_gate.shape[0]
    local_copies = owned + 1
    capacity = tok_dev * fanout // (groups * local_copies) + 2
    sizes = (owned, groups, capacity)
    rows = groups * capacity
    route_t, gate_t = route.T, gate_prob.T
    code, sends = send_rows(route_t, gate_t, tokens, cotangent, *sizes)

    weights = combine_weights(code.T, gate_prob, *sizes)
    own_pick = replica_pick[(column + groups // 2) % groups]
    place = lax.axis_index("dp")
    steps = jnp.array([0, 1, 3, 2, 0, 1, 3, 2, 0], jnp.int32)
    flip = jnp.array([0, 0, 0, 0, 1, 1, 1, 1, 0], jnp.int32)
    at = 2 * ((place // 2 + steps) % 4) + (place % 2 + flip) % 2
    at = jnp.where(jnp.arange(9) == 8, own_pick, at * width).astype(jnp.int32)

    def swap(x):
        return lax.all_to_all(x.reshape(groups, 2 * capacity, width), "expert", split_axis=0, concat_axis=0, tiled=True)

    got, math = [], []
    for part, send in enumerate(sends):
        thin = swap(send)
        thin = thin.reshape(groups, 2, capacity, width).transpose(1, 0, 2, 3).reshape(2, rows, width)
        pieces = spread(thin)
        math.append(expert_math(at, pieces, (w_gate, w_up, w_down), part, owned))
        back = gathered_sum(*math[-1][3:])
        back = back.reshape(2, groups, capacity, width).transpose(1, 0, 2, 3)
        got.append(swap(back).reshape(groups * 2 * capacity, width))
    total = sum(dot_nn(weights[part], got[part]) for part in range(local_copies))
    layer_out = (total[:tok_dev] + total[tok_dev : 2 * tok_dev]).astype(BF)
    token_grad = total[2 * tok_dev :].astype(BF)
    sums = jnp.concatenate([m[2] for m in math])
    for mask in (1, 2, 4):
        sums = sums + lax.ppermute(sums, "dp", [(i, i ^ mask) for i in range(lax.axis_size("dp"))])
    sums = sums.reshape(local_copies, groups, capacity).transpose(1, 0, 2)
    sums = sums.reshape(groups, 1, local_copies * capacity)
    sums = lax.all_to_all(sums, "expert", split_axis=0, concat_axis=0, tiled=True)
    sums = sums.reshape(groups, local_copies * capacity)
    mine = lax.dynamic_index_in_dim(code, place, 0, keepdims=False)
    copy, inside = mine // capacity, mine % capacity
    index, kind = copy // local_copies, copy % local_copies
    holder = jnp.where(kind == owned, (index + groups // 2) % groups, index)
    column_of = kind * capacity + inside
    picked = jnp.dot(
        (holder[:, None] == jnp.arange(groups)[None, :]).astype(F32), sums, precision=lax.Precision.HIGHEST
    )
    picked = jnp.where(column_of[:, None] == jnp.arange(local_copies * capacity)[None, :], picked, 0.0)
    gate_grad = picked.sum(axis=1) / lax.dynamic_index_in_dim(gate_t, place, 0, keepdims=False)

    w_gate_grad, w_up_grad, w_down_grad = grads(own_pick.reshape(1), [m[0] for m in math], [m[1] for m in math], owned)
    return (layer_out, token_grad, gate_grad.reshape(tok_dev, 1), w_gate_grad, w_up_grad, w_down_grad)


def solution(mesh):
    in_specs = (
        P("expert", "dp"),
        P("expert", "dp"),
        P("expert", None),
        P("expert", None),
        P(),
        P("expert", "dp", None),
        P("expert", "dp", None),
        P("expert", "dp", None),
    )
    out_specs = (
        P("expert", "dp"),
        P("expert", "dp"),
        P("expert", "dp"),
        P("expert", "dp", None),
        P("expert", "dp", None),
        P("expert", "dp", None),
    )

    return jax.shard_map(body, mesh=mesh, in_specs=in_specs, out_specs=out_specs, check_vma=False)
```

```python
import functools

import jax
import jax.numpy as jnp
from jax import lax
from jax.experimental import pallas as pl
from jax.experimental.pallas import tpu as pltpu
from jax.sharding import PartitionSpec as P


BF = jnp.bfloat16
F32 = jnp.float32


def row_codes(first, rows, tok_dev, part, groups, owned, capacity):
    local_copies = owned + 1
    r = first + lax.broadcasted_iota(jnp.int32, (rows, tok_dev), 0)
    wide = 2 * capacity
    group = (r.astype(F32) * (1.0 / wide) + 0.5 / wide).astype(jnp.int32)
    inside = r - group * wide
    front = inside < capacity
    place = jnp.where(front, inside, inside - capacity)
    if part < owned:
        copy = group * local_copies + part
    else:
        holder = group + groups // 2
        holder = jnp.where(holder >= groups, holder - groups, holder)
        copy = holder * local_copies + owned
    return copy * capacity + place, front


def send_kernel(owned, groups, capacity, block, route_ref, gate_ref, tok_ref, cot_ref, code_ref, *out_refs):
    fanout, tok_dev = route_ref.shape
    copies = groups * (owned + 1)
    ids = lax.broadcasted_iota(jnp.int32, (copies, tok_dev), 0)
    named = jnp.zeros((copies, tok_dev), F32)
    for k in range(fanout):
        named = jnp.where(route_ref[k : k + 1, :] == ids, 1.0, named)
    before = lax.broadcasted_iota(jnp.int32, (tok_dev, tok_dev), 0) < lax.broadcasted_iota(
        jnp.int32, (tok_dev, tok_dev), 1
    )
    rank = jnp.dot(named.astype(BF), jnp.where(before, 1.0, 0.0).astype(BF), preferred_element_type=F32)
    codes, gates = [], []
    for k in range(fanout):
        row = route_ref[k : k + 1, :]
        at = jnp.sum(jnp.where(row == ids, rank, 0.0), axis=0, keepdims=True)
        codes.append(row * capacity + at.astype(jnp.int32))
        gates.append(gate_ref[k : k + 1, :])
    code_ref[...] = jnp.concatenate(codes, axis=0)
    both = jnp.concatenate([tok_ref[...], cot_ref[...]], axis=0)
    for part, out_ref in enumerate(out_refs):
        for first in range(0, out_ref.shape[0], block):
            slot, front = row_codes(first, block, tok_dev, part, groups, owned, capacity)
            match = jnp.zeros((block, tok_dev), F32)
            scale = jnp.zeros((block, tok_dev), F32)
            for k in range(fanout):
                same = codes[k] == slot
                match = jnp.where(same, 1.0, match)
                scale = jnp.where(same, gates[k], scale)
            pick = jnp.concatenate([jnp.where(front, match, 0.0), jnp.where(front, 0.0, match)], axis=1)
            rows = jnp.dot(pick.astype(BF), both, preferred_element_type=F32)
            scale = jnp.sum(jnp.where(front, 0.0, scale), axis=1, keepdims=True)
            scale = jnp.where(front[:, :1], 1.0, scale)
            out_ref[first : first + block, :] = (rows * scale).astype(BF)


def send_rows(route_t, gate_t, tokens, cot, owned, groups, capacity):
    rows, width = groups * 2 * capacity, tokens.shape[1]
    out = pl.pallas_call(
        functools.partial(send_kernel, owned, groups, capacity, 4 * 2 * capacity),
        out_shape=[jax.ShapeDtypeStruct(route_t.shape, jnp.int32)]
        + [jax.ShapeDtypeStruct((rows, width), BF)] * (owned + 1),
        name="send_rows",
    )(route_t, gate_t, tokens, cot)
    return out[0], out[1:]


def combine_kernel(owned, groups, capacity, part, first_call, last_call, *refs):
    code_ref, gate_ref, cot_ref, got_ref = refs[:4]
    acc_ref, gp_ref = (None, None) if first_call else refs[4:6]
    outs = refs[4:] if first_call else refs[6:]
    fanout, tok_dev = code_ref.shape
    nt = (((1,), (1,)), ((), ()))
    tn = (((0,), (0,)), ((), ()))
    block = 8 * 2 * capacity

    def step(i, carried):
        acc, gp = carried
        first = i * block
        got = got_ref[first : first + block, :]
        z = lax.dot_general(got, cot_ref[...], nt, preferred_element_type=F32)
        slot, front = row_codes(first, block, tok_dev, part, groups, owned, capacity)
        match = jnp.zeros(z.shape, F32)
        scale = jnp.zeros(z.shape, F32)
        zf = jnp.where(front, z, 0.0)
        parts = []
        for k in range(fanout):
            same = code_ref[k : k + 1, :] == slot
            match = jnp.where(same, 1.0, match)
            scale = jnp.where(same, gate_ref[k : k + 1, :], scale)
            parts.append(jnp.sum(jnp.where(same, zf, 0.0), axis=0, keepdims=True))
        scale = jnp.where(front, scale, 0.0)
        high = scale.astype(BF)
        low = (scale - high.astype(F32)).astype(BF)
        back = jnp.where(front, 0.0, match).astype(BF)
        weights = jnp.concatenate([high, low, back], axis=1)
        acc = acc + lax.dot_general(weights, got, tn, preferred_element_type=F32)
        return acc, gp + jnp.concatenate(parts, axis=0)

    start = (jnp.zeros((3 * tok_dev, cot_ref.shape[1]), F32), jnp.zeros((fanout, tok_dev), F32))
    acc, gp = start
    for i in range(got_ref.shape[0] // block):
        acc, gp = step(i, (acc, gp))
    if not first_call:
        acc = acc + acc_ref[...]
        gp = gp + gp_ref[...]
    if last_call:
        outs[0][...] = (acc[:tok_dev] + acc[tok_dev : 2 * tok_dev]).astype(BF)
        outs[1][...] = acc[2 * tok_dev :].astype(BF)
        outs[2][...] = gp
    else:
        outs[0][...] = acc
        outs[1][...] = gp


def combine(code, gate_t, cot, got, carried, part, last_call, owned, groups, capacity):
    tok_dev, width = cot.shape
    gp_shape = jax.ShapeDtypeStruct(code.shape, F32)
    if last_call:
        out_shape = [jax.ShapeDtypeStruct((tok_dev, width), BF)] * 2 + [gp_shape]
    else:
        out_shape = [jax.ShapeDtypeStruct((3 * tok_dev, width), F32), gp_shape]
    return pl.pallas_call(
        functools.partial(combine_kernel, owned, groups, capacity, part, not carried, last_call), out_shape=out_shape
    )(code, gate_t, cot, got, *carried)


def dot_nt(x, w):
    return lax.dot_general(x, w, (((1,), (1,)), ((), ())), preferred_element_type=F32)


def dot_nn(x, w):
    return jnp.dot(x, w, preferred_element_type=F32)


def math_kernel(width, at_ref, in_ref, cot_ref, gate_ref, up_ref, down_ref, acts_ref, *outs):
    gate_act = dot_nt(in_ref[...], gate_ref[0])
    up_act = dot_nt(in_ref[...], up_ref[0])
    d_hidden = dot_nt(cot_ref[...], down_ref[0])
    s = jax.nn.sigmoid(gate_act)
    activated = gate_act * s
    hidden = activated * up_act
    d_gate = d_hidden * up_act * s * (1.0 + gate_act * (1.0 - s))
    d_up = d_hidden * activated
    for n, act in enumerate((hidden, d_gate, d_up)):
        acts_ref[n] = act.T.astype(BF)
    hidden, d_gate, d_up = hidden.astype(BF), d_gate.astype(BF), d_up.astype(BF)
    for q, (ref, n) in enumerate(
        ((outs[0], 0), (outs[0], 1), (outs[0], 2), (outs[1], None), (outs[2], 0), (outs[2], 1), (outs[2], 2), (outs[3], None))
    ):
        at = pl.ds(pl.multiple_of(at_ref[q], width), width)
        out = dot_nn(hidden, down_ref[0, :, at]).astype(BF)
        back = (dot_nn(d_gate, gate_ref[0, :, at]) + dot_nn(d_up, up_ref[0, :, at])).astype(BF)
        where = () if n is None else (n,)
        ref[(*where, 0)] = out
        ref[(*where, 1)] = back


def expert_math(at, wide, slot, weights, part, owned, width):
    rows = wide.shape[0] // 2 if part == 0 else wide.shape[0] // 2 // owned
    hidden, features = weights[0].shape[1:]

    def whole(shape):
        return pl.BlockSpec(shape, lambda i, at: (0,) * len(shape))

    if part < owned:
        w_spec = pl.BlockSpec((1, hidden, features), lambda i, at: (part, 0, 0))
    else:
        w_spec = pl.BlockSpec((1, hidden, features), lambda i, at: (at[8], 0, 0))
    out_shape = [
        jax.ShapeDtypeStruct(shape, BF)
        for shape in (
            (3, hidden, rows),
            (3, 2, rows, width),
            (2, rows, width),
            (3, 2, rows, width),
            (2, rows, width),
        )
    ]
    return pl.pallas_call(
        functools.partial(math_kernel, width),
        grid_spec=pltpu.PrefetchScalarGridSpec(
            num_scalar_prefetch=1,
            grid=(1,),
            in_specs=[
                pl.BlockSpec((rows, features), lambda i, at: (slot, 0)),
                pl.BlockSpec((rows, features), lambda i, at: (slot + 1, 0)),
            ]
            + [w_spec] * 3,
            out_specs=[whole(o.shape) for o in out_shape],
        ),
        out_shape=out_shape,
        compiler_params=pltpu.CompilerParams(vmem_limit_bytes=56 * 1024 * 1024),
    )(at, wide, wide, *weights)


def grads_kernel(owned, pick_ref, *refs):
    n_parts = owned + 1
    wide, acts, outs = refs[: 2 * n_parts], refs[2 * n_parts : 3 * n_parts], refs[3 * n_parts :]
    for out_ref, n, which in zip(outs, (1, 2, 0), (0, 0, 1)):
        extra = dot_nn(acts[owned][n], wide[2 * owned + which][...])
        for i in range(owned):
            keep = jnp.where(pick_ref[0] == i, 1.0, 0.0)
            out_ref[i] = (dot_nn(acts[i][n], wide[2 * i + which][...]) + keep * extra).astype(BF)


def grads(pick, wide, slots, acts, owned):
    features = wide[0].shape[1]
    hidden, rows = acts[0].shape[1:]
    block = features // 4
    specs, args = [], []
    for array, slot in zip(wide, slots):
        for which in range(2):
            specs.append(pl.BlockSpec((rows, block), lambda i, p, at=slot + which: (at, i)))
            args.append(array)
    return pl.pallas_call(
        functools.partial(grads_kernel, owned),
        grid_spec=pltpu.PrefetchScalarGridSpec(
            num_scalar_prefetch=1,
            grid=(features // block,),
            in_specs=specs + [pl.BlockSpec((3, hidden, rows), lambda i, p: (0, 0, 0))] * (owned + 1),
            out_specs=[pl.BlockSpec((owned, hidden, block), lambda i, p: (0, 0, i))] * 3,
        ),
        out_shape=[jax.ShapeDtypeStruct((owned, hidden, features), BF)] * 3,
        compiler_params=pltpu.CompilerParams(vmem_limit_bytes=56 * 1024 * 1024),
        name="weight_grads",
    )(pick, *args, *acts)


def hop(x, by):
    n = lax.axis_size("dp")
    return lax.ppermute(x, "dp", [(i, (i + 2 * by) % n) for i in range(n)])


def twin(x):
    return lax.ppermute(x, "dp", [(i, i ^ 1) for i in range(lax.axis_size("dp"))])


def gathered_sum(near, near_opp, far, far_opp):
    both_opp = (near_opp.astype(F32) + twin(far_opp).astype(F32)).astype(BF)
    both = near.astype(F32) + twin(far).astype(F32)
    from_left = hop(both_opp[0], 1).astype(F32)
    from_right = hop(both_opp[1], -1).astype(F32)
    to_right = jnp.stack([both[1, 0] + from_left, both[1, 1]]).astype(BF)
    to_left = jnp.stack([both[2, 0], both[2, 1] + from_right]).astype(BF)
    to_left, to_right = hop(to_left, -1), hop(to_right, 1)
    return (both[0] + to_right.astype(F32) + to_left.astype(F32)).astype(BF)


def body(tokens, cotangent, route, gate_prob, replica_pick, w_gate, w_up, w_down):
    groups = lax.axis_size("expert")
    column = lax.axis_index("expert")
    tok_dev, width = tokens.shape
    fanout = route.shape[1]
    owned = w_gate.shape[0]
    local_copies = owned + 1
    capacity = tok_dev * fanout // (groups * local_copies) + 2
    sizes = (owned, groups, capacity)
    rows = groups * capacity
    route_t, gate_t = route.T, gate_prob.T
    code, sends = send_rows(route_t, gate_t, tokens, cotangent, *sizes)

    own_pick = replica_pick[(column + groups // 2) % groups]
    place = lax.axis_index("dp")
    steps = jnp.array([0, 1, 3, 2, 0, 1, 3, 2, 0], jnp.int32)
    flip = jnp.array([0, 0, 0, 0, 1, 1, 1, 1, 0], jnp.int32)
    at = 2 * ((place // 2 + steps) % 4) + (place % 2 + flip) % 2
    at = jnp.where(jnp.arange(9) == 8, own_pick, at * width).astype(jnp.int32)

    def swap(x):
        x = x.reshape(groups, -1, width)
        return lax.all_to_all(x, "expert", split_axis=0, concat_axis=0, tiled=True)

    def gather(send):
        parts = send.shape[1] // (2 * capacity)
        thin = swap(send).reshape(groups, 2 * parts, capacity, width)
        thin = thin.transpose(1, 0, 2, 3).reshape(2 * parts * rows, width)
        return lax.all_gather(thin, "dp", axis=1, tiled=True)

    wide_first = gather(sends[0].reshape(groups, -1, width))
    wide_rest = gather(jnp.concatenate([send.reshape(groups, -1, width) for send in sends[1:]], axis=1))
    wide = [wide_first] + [wide_rest] * owned
    slots = [0] + [2 * n for n in range(owned)]
    got, math = [], []
    for part in range(local_copies):
        math.append(
            expert_math(at, wide[part], slots[part], (w_gate, w_up, w_down), part, owned, width)
        )
        back = gathered_sum(*math[-1][1:])
        back = back.reshape(2, groups, capacity, width).transpose(1, 0, 2, 3)
        got.append(swap(back).reshape(groups * 2 * capacity, width))
    carried = ()
    for part in range(local_copies):
        carried = combine(code, gate_t, cotangent, got[part], carried, part, part == owned, *sizes)
    layer_out, token_grad, gate_part = carried
    gate_grad = lax.all_to_all(
        gate_part.reshape(fanout, 1, tok_dev), "dp", split_axis=0, concat_axis=0, tiled=True
    ).sum(axis=0)

    w_gate_grad, w_up_grad, w_down_grad = grads(
        own_pick.reshape(1), wide, slots, [m[0] for m in math], owned
    )
    return (layer_out, token_grad, gate_grad.reshape(tok_dev, 1), w_gate_grad, w_up_grad, w_down_grad)


def solution(mesh):
    in_specs = (
        P("expert", "dp"),
        P("expert", "dp"),
        P("expert", None),
        P("expert", None),
        P(),
        P("expert", "dp", None),
        P("expert", "dp", None),
        P("expert", "dp", None),
    )
    out_specs = (
        P("expert", "dp"),
        P("expert", "dp"),
        P("expert", "dp"),
        P("expert", "dp", None),
        P("expert", "dp", None),
        P("expert", "dp", None),
    )

    return jax.shard_map(body, mesh=mesh, in_specs=in_specs, out_specs=out_specs, check_vma=False)
```

```python
import functools

import jax
import jax.numpy as jnp
from jax import lax
from jax.experimental import pallas as pl
from jax.experimental.pallas import tpu as pltpu
from jax.sharding import PartitionSpec as P


BF = jnp.bfloat16
F32 = jnp.float32


def row_codes(first, shape, axis, part, groups, owned, capacity):
    local_copies = owned + 1
    r = first + lax.broadcasted_iota(jnp.int32, shape, axis)
    wide = 2 * capacity
    group = (r.astype(F32) * (1.0 / wide) + 0.5 / wide).astype(jnp.int32)
    inside = r - group * wide
    front = inside < capacity
    place = jnp.where(front, inside, inside - capacity)
    if part < owned:
        copy = group * local_copies + part
    else:
        holder = group + groups // 2
        holder = jnp.where(holder >= groups, holder - groups, holder)
        copy = holder * local_copies + owned
    return copy * capacity + place, front


def send_kernel(owned, groups, capacity, block, route_ref, gate_ref, tok_ref, cot_ref, code_ref, *out_refs):
    fanout, tok_dev = route_ref.shape
    copies = groups * (owned + 1)
    ids = lax.broadcasted_iota(jnp.int32, (copies, tok_dev), 0)
    named = jnp.zeros((copies, tok_dev), F32)
    for k in range(fanout):
        named = jnp.where(route_ref[k : k + 1, :] == ids, 1.0, named)
    before = lax.broadcasted_iota(jnp.int32, (tok_dev, tok_dev), 0) < lax.broadcasted_iota(
        jnp.int32, (tok_dev, tok_dev), 1
    )
    rank = jnp.dot(named.astype(BF), jnp.where(before, 1.0, 0.0).astype(BF), preferred_element_type=F32)
    codes, gates = [], []
    for k in range(fanout):
        row = route_ref[k : k + 1, :]
        at = jnp.sum(jnp.where(row == ids, rank, 0.0), axis=0, keepdims=True)
        codes.append(row * capacity + at.astype(jnp.int32))
        gates.append(gate_ref[k : k + 1, :])
    code_ref[...] = jnp.concatenate(codes, axis=0)
    both = jnp.concatenate([tok_ref[...], cot_ref[...]], axis=0)
    for part, out_ref in enumerate(out_refs):
        for first in range(0, out_ref.shape[0], block):
            slot, front = row_codes(first, (block, tok_dev), 0, part, groups, owned, capacity)
            match = jnp.zeros((block, tok_dev), F32)
            scale = jnp.zeros((block, tok_dev), F32)
            for k in range(fanout):
                same = codes[k] == slot
                match = jnp.where(same, 1.0, match)
                scale = jnp.where(same, gates[k], scale)
            pick = jnp.concatenate([jnp.where(front, match, 0.0), jnp.where(front, 0.0, match)], axis=1)
            rows = jnp.dot(pick.astype(BF), both, preferred_element_type=F32)
            scale = jnp.sum(jnp.where(front, 0.0, scale), axis=1, keepdims=True)
            scale = jnp.where(front[:, :1], 1.0, scale)
            out_ref[first : first + block, :] = (rows * scale).astype(BF)


def send_rows(route_t, gate_t, tokens, cot, owned, groups, capacity):
    rows, width = groups * 2 * capacity, tokens.shape[1]
    out = pl.pallas_call(
        functools.partial(send_kernel, owned, groups, capacity, 4 * 2 * capacity),
        out_shape=[jax.ShapeDtypeStruct(route_t.shape, jnp.int32)]
        + [jax.ShapeDtypeStruct((rows, width), BF)] * (owned + 1),
        name="send_rows",
    )(route_t, gate_t, tokens, cot)
    return out[0], out[1:]


def weights_kernel(owned, groups, capacity, code_ref, gate_ref, out_ref):
    tok_dev, fanout = code_ref.shape
    lanes = 128
    for part in range(owned + 1):
        @pl.loop(0, out_ref.shape[2] // lanes)
        def _(i, part=part):
            first = pl.multiple_of(i * lanes, lanes)
            slot, front = row_codes(first, (tok_dev, lanes), 1, part, groups, owned, capacity)
            match = jnp.zeros((tok_dev, lanes), F32)
            scale = jnp.zeros((tok_dev, lanes), F32)
            for k in range(fanout):
                same = code_ref[:, k : k + 1] == slot
                match = jnp.where(same, 1.0, match)
                scale = jnp.where(same, gate_ref[:, k : k + 1], scale)
            scale = jnp.where(front, scale, 0.0)
            high = scale.astype(BF)
            out_ref[part, :tok_dev, pl.ds(first, lanes)] = high
            out_ref[part, tok_dev : 2 * tok_dev, pl.ds(first, lanes)] = (scale - high.astype(F32)).astype(BF)
            out_ref[part, 2 * tok_dev :, pl.ds(first, lanes)] = jnp.where(front, 0.0, match).astype(BF)


def combine_weights(code, gate, owned, groups, capacity):
    tok_dev = code.shape[0]
    return pl.pallas_call(
        functools.partial(weights_kernel, owned, groups, capacity),
        out_shape=jax.ShapeDtypeStruct((owned + 1, 3 * tok_dev, groups * 2 * capacity), BF),
        name="combine_weights",
    )(code, gate)


def dot_nt(x, w):
    return lax.dot_general(x, w, (((1,), (1,)), ((), ())), preferred_element_type=F32)


def dot_nn(x, w):
    return jnp.dot(x, w, preferred_element_type=F32)


def math_kernel(width, at_ref, in_ref, cot_ref, gate_ref, up_ref, down_ref, acts_ref, sums_ref, *outs):
    gate_act = dot_nt(in_ref[...], gate_ref[0])
    up_act = dot_nt(in_ref[...], up_ref[0])
    d_hidden = dot_nt(cot_ref[...], down_ref[0])
    s = jax.nn.sigmoid(gate_act)
    activated = gate_act * s
    hidden = activated * up_act
    d_gate = d_hidden * up_act * s * (1.0 + gate_act * (1.0 - s))
    d_up = d_hidden * activated
    sums_ref[...] = jnp.sum((hidden.astype(BF).astype(F32) * d_hidden).T, axis=0, keepdims=True)
    for n, act in enumerate((hidden, d_gate, d_up)):
        acts_ref[n] = act.T.astype(BF)
    hidden, d_gate, d_up = hidden.astype(BF), d_gate.astype(BF), d_up.astype(BF)
    for q, (ref, n) in enumerate(
        ((outs[0], 0), (outs[0], 1), (outs[0], 2), (outs[1], None), (outs[2], 0), (outs[2], 1), (outs[2], 2), (outs[3], None))
    ):
        at = pl.ds(pl.multiple_of(at_ref[q], width), width)
        out = dot_nn(hidden, down_ref[0, :, at]).astype(BF)
        back = (dot_nn(d_gate, gate_ref[0, :, at]) + dot_nn(d_up, up_ref[0, :, at])).astype(BF)
        where = () if n is None else (n,)
        ref[(*where, 0)] = out
        ref[(*where, 1)] = back


def expert_math(at, wide, weights, part, owned, width):
    rows = wide.shape[0] // 2
    hidden, features = weights[0].shape[1:]

    def whole(shape):
        return pl.BlockSpec(shape, lambda i, at: (0,) * len(shape))

    if part < owned:
        w_spec = pl.BlockSpec((1, hidden, features), lambda i, at: (part, 0, 0))
    else:
        w_spec = pl.BlockSpec((1, hidden, features), lambda i, at: (at[8], 0, 0))
    out_shape = [
        jax.ShapeDtypeStruct(shape, BF)
        for shape in (
            (3, hidden, rows),
            (1, rows),
            (3, 2, rows, width),
            (2, rows, width),
            (3, 2, rows, width),
            (2, rows, width),
        )
    ]
    out_shape[1] = jax.ShapeDtypeStruct((1, rows), F32)
    return pl.pallas_call(
        functools.partial(math_kernel, width),
        grid_spec=pltpu.PrefetchScalarGridSpec(
            num_scalar_prefetch=1,
            grid=(1,),
            in_specs=[
                pl.BlockSpec((rows, features), lambda i, at: (0, 0)),
                pl.BlockSpec((rows, features), lambda i, at: (1, 0)),
            ]
            + [w_spec] * 3,
            out_specs=[whole(o.shape) for o in out_shape],
        ),
        out_shape=out_shape,
        compiler_params=pltpu.CompilerParams(vmem_limit_bytes=56 * 1024 * 1024),
    )(at, wide, wide, *weights)


def grads_kernel(owned, pick_ref, *refs):
    n_parts = owned + 1
    wide, acts, outs = refs[: 2 * n_parts], refs[2 * n_parts : 3 * n_parts], refs[3 * n_parts :]
    for out_ref, n, which in zip(outs, (1, 2, 0), (0, 0, 1)):
        extra = dot_nn(acts[owned][n], wide[2 * owned + which][...])
        for i in range(owned):
            keep = jnp.where(pick_ref[0] == i, 1.0, 0.0)
            out_ref[i] = (dot_nn(acts[i][n], wide[2 * i + which][...]) + keep * extra).astype(BF)


def grads(pick, wide, acts, owned):
    features = wide[0].shape[1]
    hidden, rows = acts[0].shape[1:]
    block = features // 4
    specs, args = [], []
    for array in wide:
        for which in range(2):
            specs.append(pl.BlockSpec((rows, block), lambda i, p, which=which: (which, i)))
            args.append(array)
    return pl.pallas_call(
        functools.partial(grads_kernel, owned),
        grid_spec=pltpu.PrefetchScalarGridSpec(
            num_scalar_prefetch=1,
            grid=(features // block,),
            in_specs=specs + [pl.BlockSpec((3, hidden, rows), lambda i, p: (0, 0, 0))] * (owned + 1),
            out_specs=[pl.BlockSpec((owned, hidden, block), lambda i, p: (0, 0, i))] * 3,
        ),
        out_shape=[jax.ShapeDtypeStruct((owned, hidden, features), BF)] * 3,
        compiler_params=pltpu.CompilerParams(vmem_limit_bytes=56 * 1024 * 1024),
        name="weight_grads",
    )(pick, *args, *acts)


def hop(x, by):
    n = lax.axis_size("dp")
    return lax.ppermute(x, "dp", [(i, (i + 2 * by) % n) for i in range(n)])


def twin(x):
    return lax.ppermute(x, "dp", [(i, i ^ 1) for i in range(lax.axis_size("dp"))])


def gathered_sum(near, near_opp, far, far_opp):
    both_opp = (near_opp.astype(F32) + twin(far_opp).astype(F32)).astype(BF)
    both = near.astype(F32) + twin(far).astype(F32)
    from_left = hop(both_opp[0], 1).astype(F32)
    from_right = hop(both_opp[1], -1).astype(F32)
    to_right = jnp.stack([both[1, 0] + from_left, both[1, 1]]).astype(BF)
    to_left = jnp.stack([both[2, 0], both[2, 1] + from_right]).astype(BF)
    to_left, to_right = hop(to_left, -1), hop(to_right, 1)
    return (both[0] + to_right.astype(F32) + to_left.astype(F32)).astype(BF)


def body(tokens, cotangent, route, gate_prob, replica_pick, w_gate, w_up, w_down):
    groups = lax.axis_size("expert")
    column = lax.axis_index("expert")
    tok_dev, width = tokens.shape
    fanout = route.shape[1]
    owned = w_gate.shape[0]
    local_copies = owned + 1
    capacity = tok_dev * fanout // (groups * local_copies) + 2
    sizes = (owned, groups, capacity)
    rows = groups * capacity
    route_t, gate_t = route.T, gate_prob.T
    code, sends = send_rows(route_t, gate_t, tokens, cotangent, *sizes)

    weights = combine_weights(code.T, gate_prob, *sizes)
    own_pick = replica_pick[(column + groups // 2) % groups]
    place = lax.axis_index("dp")
    steps = jnp.array([0, 1, 3, 2, 0, 1, 3, 2, 0], jnp.int32)
    flip = jnp.array([0, 0, 0, 0, 1, 1, 1, 1, 0], jnp.int32)
    at = 2 * ((place // 2 + steps) % 4) + (place % 2 + flip) % 2
    at = jnp.where(jnp.arange(9) == 8, own_pick, at * width).astype(jnp.int32)

    def swap(x):
        x = x.reshape(groups, -1, width)
        return lax.all_to_all(x, "expert", split_axis=0, concat_axis=0, tiled=True)

    def gather(send):
        thin = swap(send).reshape(groups, 2, capacity, width)
        thin = thin.transpose(1, 0, 2, 3).reshape(2 * rows, width)
        return lax.all_gather(thin, "dp", axis=1, tiled=True)

    wide, got, math = [], [], []
    for part, send in enumerate(sends):
        wide.append(gather(send))
        math.append(expert_math(at, wide[part], (w_gate, w_up, w_down), part, owned, width))
        back = gathered_sum(*math[-1][2:])
        back = back.reshape(2, groups, capacity, width).transpose(1, 0, 2, 3)
        got.append(swap(back).reshape(groups * 2 * capacity, width))
    total = sum(dot_nn(weights[part], got[part]) for part in range(local_copies))
    layer_out = (total[:tok_dev] + total[tok_dev : 2 * tok_dev]).astype(BF)
    token_grad = total[2 * tok_dev :].astype(BF)
    sums = jnp.concatenate([m[1] for m in math])
    for mask in (1, 2, 4):
        sums = sums + lax.ppermute(sums, "dp", [(i, i ^ mask) for i in range(lax.axis_size("dp"))])
    sums = sums.reshape(local_copies, groups, capacity).transpose(1, 0, 2)
    sums = sums.reshape(groups, 1, local_copies * capacity)
    sums = lax.all_to_all(sums, "expert", split_axis=0, concat_axis=0, tiled=True)
    sums = sums.reshape(groups, local_copies * capacity)
    mine = lax.dynamic_index_in_dim(code, place, 0, keepdims=False)
    copy, inside = mine // capacity, mine % capacity
    index, kind = copy // local_copies, copy % local_copies
    holder = jnp.where(kind == owned, (index + groups // 2) % groups, index)
    column_of = kind * capacity + inside
    picked = jnp.dot(
        (holder[:, None] == jnp.arange(groups)[None, :]).astype(F32), sums, precision=lax.Precision.HIGHEST
    )
    picked = jnp.where(column_of[:, None] == jnp.arange(local_copies * capacity)[None, :], picked, 0.0)
    gate_grad = picked.sum(axis=1) / lax.dynamic_index_in_dim(gate_t, place, 0, keepdims=False)

    w_gate_grad, w_up_grad, w_down_grad = grads(
        own_pick.reshape(1), wide, [m[0] for m in math], owned
    )
    return (layer_out, token_grad, gate_grad.reshape(tok_dev, 1), w_gate_grad, w_up_grad, w_down_grad)


def solution(mesh):
    in_specs = (
        P("expert", "dp"),
        P("expert", "dp"),
        P("expert", None),
        P("expert", None),
        P(),
        P("expert", "dp", None),
        P("expert", "dp", None),
        P("expert", "dp", None),
    )
    out_specs = (
        P("expert", "dp"),
        P("expert", "dp"),
        P("expert", "dp"),
        P("expert", "dp", None),
        P("expert", "dp", None),
        P("expert", "dp", None),
    )

    return jax.shard_map(body, mesh=mesh, in_specs=in_specs, out_specs=out_specs, check_vma=False)
```

```python
import functools

import jax
import jax.numpy as jnp
from jax import lax
from jax.experimental import pallas as pl
from jax.experimental.pallas import tpu as pltpu
from jax.sharding import PartitionSpec as P


BF = jnp.bfloat16
F32 = jnp.float32


def row_codes(first, rows, tok_dev, part, groups, owned, capacity):
    local_copies = owned + 1
    r = first + lax.broadcasted_iota(jnp.int32, (rows, tok_dev), 0)
    wide = 2 * capacity
    group = (r.astype(F32) * (1.0 / wide) + 0.5 / wide).astype(jnp.int32)
    inside = r - group * wide
    front = inside < capacity
    place = jnp.where(front, inside, inside - capacity)
    if part < owned:
        copy = group * local_copies + part
    else:
        holder = group + groups // 2
        holder = jnp.where(holder >= groups, holder - groups, holder)
        copy = holder * local_copies + owned
    return copy * capacity + place, front


def send_kernel(owned, groups, capacity, block, route_ref, gate_ref, tok_ref, cot_ref, code_ref, *out_refs):
    fanout, tok_dev = route_ref.shape
    copies = groups * (owned + 1)
    ids = lax.broadcasted_iota(jnp.int32, (copies, tok_dev), 0)
    named = jnp.zeros((copies, tok_dev), F32)
    for k in range(fanout):
        named = jnp.where(route_ref[k : k + 1, :] == ids, 1.0, named)
    before = lax.broadcasted_iota(jnp.int32, (tok_dev, tok_dev), 0) < lax.broadcasted_iota(
        jnp.int32, (tok_dev, tok_dev), 1
    )
    rank = jnp.dot(named.astype(BF), jnp.where(before, 1.0, 0.0).astype(BF), preferred_element_type=F32)
    codes, gates = [], []
    for k in range(fanout):
        row = route_ref[k : k + 1, :]
        at = jnp.sum(jnp.where(row == ids, rank, 0.0), axis=0, keepdims=True)
        codes.append(row * capacity + at.astype(jnp.int32))
        gates.append(gate_ref[k : k + 1, :])
    code_ref[...] = jnp.concatenate(codes, axis=0)
    both = jnp.concatenate([tok_ref[...], cot_ref[...]], axis=0)
    for part, out_ref in enumerate(out_refs):
        for first in range(0, out_ref.shape[0], block):
            slot, front = row_codes(first, block, tok_dev, part, groups, owned, capacity)
            match = jnp.zeros((block, tok_dev), F32)
            scale = jnp.zeros((block, tok_dev), F32)
            for k in range(fanout):
                same = codes[k] == slot
                match = jnp.where(same, 1.0, match)
                scale = jnp.where(same, gates[k], scale)
            pick = jnp.concatenate([jnp.where(front, match, 0.0), jnp.where(front, 0.0, match)], axis=1)
            rows = jnp.dot(pick.astype(BF), both, preferred_element_type=F32)
            scale = jnp.sum(jnp.where(front, 0.0, scale), axis=1, keepdims=True)
            scale = jnp.where(front[:, :1], 1.0, scale)
            out_ref[first : first + block, :] = (rows * scale).astype(BF)


def send_rows(route_t, gate_t, tokens, cot, owned, groups, capacity):
    rows, width = groups * 2 * capacity, tokens.shape[1]
    out = pl.pallas_call(
        functools.partial(send_kernel, owned, groups, capacity, 4 * 2 * capacity),
        out_shape=[jax.ShapeDtypeStruct(route_t.shape, jnp.int32)]
        + [jax.ShapeDtypeStruct((rows, width), BF)] * (owned + 1),
        name="send_rows",
    )(route_t, gate_t, tokens, cot)
    return out[0], out[1:]


def combine_kernel(owned, groups, capacity, part, first_call, last_call, *refs):
    code_ref, gate_ref, cot_ref, got_ref = refs[:4]
    acc_ref, gp_ref = (None, None) if first_call else refs[4:6]
    outs = refs[4:] if first_call else refs[6:]
    fanout, tok_dev = code_ref.shape
    nt = (((1,), (1,)), ((), ()))
    tn = (((0,), (0,)), ((), ()))
    block = 8 * 2 * capacity

    def step(i, carried):
        acc, gp = carried
        first = i * block
        got = got_ref[first : first + block, :]
        z = lax.dot_general(got, cot_ref[...], nt, preferred_element_type=F32)
        slot, front = row_codes(first, block, tok_dev, part, groups, owned, capacity)
        match = jnp.zeros(z.shape, F32)
        scale = jnp.zeros(z.shape, F32)
        zf = jnp.where(front, z, 0.0)
        parts = []
        for k in range(fanout):
            same = code_ref[k : k + 1, :] == slot
            match = jnp.where(same, 1.0, match)
            scale = jnp.where(same, gate_ref[k : k + 1, :], scale)
            parts.append(jnp.sum(jnp.where(same, zf, 0.0), axis=0, keepdims=True))
        scale = jnp.where(front, scale, 0.0)
        high = scale.astype(BF)
        low = (scale - high.astype(F32)).astype(BF)
        back = jnp.where(front, 0.0, match).astype(BF)
        weights = jnp.concatenate([high, low, back], axis=1)
        acc = acc + lax.dot_general(weights, got, tn, preferred_element_type=F32)
        return acc, gp + jnp.concatenate(parts, axis=0)

    start = (jnp.zeros((3 * tok_dev, cot_ref.shape[1]), F32), jnp.zeros((fanout, tok_dev), F32))
    acc, gp = start
    for i in range(got_ref.shape[0] // block):
        acc, gp = step(i, (acc, gp))
    if not first_call:
        acc = acc + acc_ref[...]
        gp = gp + gp_ref[...]
    if last_call:
        outs[0][...] = (acc[:tok_dev] + acc[tok_dev : 2 * tok_dev]).astype(BF)
        outs[1][...] = acc[2 * tok_dev :].astype(BF)
        outs[2][...] = gp
    else:
        outs[0][...] = acc
        outs[1][...] = gp


def combine(code, gate_t, cot, got, carried, part, last_call, owned, groups, capacity):
    tok_dev, width = cot.shape
    gp_shape = jax.ShapeDtypeStruct(code.shape, F32)
    if last_call:
        out_shape = [jax.ShapeDtypeStruct((tok_dev, width), BF)] * 2 + [gp_shape]
    else:
        out_shape = [jax.ShapeDtypeStruct((3 * tok_dev, width), F32), gp_shape]
    return pl.pallas_call(
        functools.partial(combine_kernel, owned, groups, capacity, part, not carried, last_call), out_shape=out_shape
    )(code, gate_t, cot, got, *carried)


def dot_nt(x, w):
    return lax.dot_general(x, w, (((1,), (1,)), ((), ())), preferred_element_type=F32)


def dot_nn(x, w):
    return jnp.dot(x, w, preferred_element_type=F32)


def math_kernel(width, at_ref, in_ref, cot_ref, gate_ref, up_ref, down_ref, acts_ref, *outs):
    gate_act = dot_nt(in_ref[...], gate_ref[0])
    up_act = dot_nt(in_ref[...], up_ref[0])
    d_hidden = dot_nt(cot_ref[...], down_ref[0])
    s = jax.nn.sigmoid(gate_act)
    activated = gate_act * s
    hidden = activated * up_act
    d_gate = d_hidden * up_act * s * (1.0 + gate_act * (1.0 - s))
    d_up = d_hidden * activated
    for n, act in enumerate((hidden, d_gate, d_up)):
        acts_ref[n] = act.T.astype(BF)
    hidden, d_gate, d_up = hidden.astype(BF), d_gate.astype(BF), d_up.astype(BF)
    for q, (ref, n) in enumerate(
        ((outs[0], 0), (outs[0], 1), (outs[0], 2), (outs[1], None), (outs[2], 0), (outs[2], 1), (outs[2], 2), (outs[3], None))
    ):
        at = pl.ds(pl.multiple_of(at_ref[q], width), width)
        out = dot_nn(hidden, down_ref[0, :, at]).astype(BF)
        back = (dot_nn(d_gate, gate_ref[0, :, at]) + dot_nn(d_up, up_ref[0, :, at])).astype(BF)
        where = () if n is None else (n,)
        ref[(*where, 0)] = out
        ref[(*where, 1)] = back


def expert_math(at, wide, weights, part, owned, width):
    rows = wide.shape[0] // 2
    hidden, features = weights[0].shape[1:]

    def whole(shape):
        return pl.BlockSpec(shape, lambda i, at: (0,) * len(shape))

    if part < owned:
        w_spec = pl.BlockSpec((1, hidden, features), lambda i, at: (part, 0, 0))
    else:
        w_spec = pl.BlockSpec((1, hidden, features), lambda i, at: (at[8], 0, 0))
    out_shape = [
        jax.ShapeDtypeStruct(shape, BF)
        for shape in (
            (3, hidden, rows),
            (3, 2, rows, width),
            (2, rows, width),
            (3, 2, rows, width),
            (2, rows, width),
        )
    ]
    return pl.pallas_call(
        functools.partial(math_kernel, width),
        grid_spec=pltpu.PrefetchScalarGridSpec(
            num_scalar_prefetch=1,
            grid=(1,),
            in_specs=[
                pl.BlockSpec((rows, features), lambda i, at: (0, 0)),
                pl.BlockSpec((rows, features), lambda i, at: (1, 0)),
            ]
            + [w_spec] * 3,
            out_specs=[whole(o.shape) for o in out_shape],
        ),
        out_shape=out_shape,
        compiler_params=pltpu.CompilerParams(vmem_limit_bytes=56 * 1024 * 1024),
    )(at, wide, wide, *weights)


def ring_math_kernel(width, at_ref, *refs):
    own, right, left, opp_in, opp_cot, p_own, p_right, p_left, p_opp_in, p_opp_cot = refs[:10]
    gate_ref, up_ref, down_ref, all_ref, acts_ref = refs[10:15]
    outs = refs[15:]
    for q, piece in ((0, own), (1, right), (2, left), (4, p_own), (5, p_right), (6, p_left)):
        all_ref[:, :, pl.ds(pl.multiple_of(at_ref[q], width), width)] = piece[...]
    for q, halves in ((3, (opp_in, opp_cot)), (7, (p_opp_in, p_opp_cot))):
        for h in range(2):
            all_ref[h, :, pl.ds(pl.multiple_of(at_ref[q], width), width)] = halves[h][...]
    gate_act = dot_nt(all_ref[0], gate_ref[0])
    up_act = dot_nt(all_ref[0], up_ref[0])
    d_hidden = dot_nt(all_ref[1], down_ref[0])
    s = jax.nn.sigmoid(gate_act)
    activated = gate_act * s
    hidden = activated * up_act
    d_gate = d_hidden * up_act * s * (1.0 + gate_act * (1.0 - s))
    d_up = d_hidden * activated
    for n, act in enumerate((hidden, d_gate, d_up)):
        acts_ref[n] = act.T.astype(BF)
    hidden, d_gate, d_up = hidden.astype(BF), d_gate.astype(BF), d_up.astype(BF)
    for q, (ref, n) in enumerate(
        ((outs[0], 0), (outs[0], 1), (outs[0], 2), (outs[1], None), (outs[2], 0), (outs[2], 1), (outs[2], 2), (outs[3], None))
    ):
        at = pl.ds(pl.multiple_of(at_ref[q], width), width)
        out = dot_nn(hidden, down_ref[0, :, at]).astype(BF)
        back = (dot_nn(d_gate, gate_ref[0, :, at]) + dot_nn(d_up, up_ref[0, :, at])).astype(BF)
        where = () if n is None else (n,)
        ref[(*where, 0)] = out
        ref[(*where, 1)] = back


def ring_math(at, pieces, weights, part, owned):
    rows, width = pieces[3].shape
    features = weights[0].shape[2]
    hidden = weights[0].shape[1]

    def whole(shape):
        return pl.BlockSpec(shape, lambda i, at: (0,) * len(shape))

    if part < owned:
        w_spec = pl.BlockSpec((1, hidden, features), lambda i, at: (part, 0, 0))
    else:
        w_spec = pl.BlockSpec((1, hidden, features), lambda i, at: (at[8], 0, 0))
    out_shape = [
        jax.ShapeDtypeStruct(shape, BF)
        for shape in (
            (2, rows, features),
            (3, hidden, rows),
            (3, 2, rows, width),
            (2, rows, width),
            (3, 2, rows, width),
            (2, rows, width),
        )
    ]
    return pl.pallas_call(
        functools.partial(ring_math_kernel, width),
        grid_spec=pltpu.PrefetchScalarGridSpec(
            num_scalar_prefetch=1,
            grid=(1,),
            in_specs=[whole(p.shape) for p in pieces] + [w_spec] * 3,
            out_specs=[whole(o.shape) for o in out_shape],
        ),
        out_shape=out_shape,
        compiler_params=pltpu.CompilerParams(vmem_limit_bytes=56 * 1024 * 1024),
    )(at, *pieces, *weights)


def grads_kernel(owned, pick_ref, *refs):
    n_parts = owned + 1
    wide, acts, outs = refs[: 2 * n_parts], refs[2 * n_parts : 3 * n_parts], refs[3 * n_parts :]
    for out_ref, n, which in zip(outs, (1, 2, 0), (0, 0, 1)):
        extra = dot_nn(acts[owned][n], wide[2 * owned + which][...])
        for i in range(owned):
            keep = jnp.where(pick_ref[0] == i, 1.0, 0.0)
            out_ref[i] = (dot_nn(acts[i][n], wide[2 * i + which][...]) + keep * extra).astype(BF)


def grads(pick, wide, acts, owned):
    features = wide[0].shape[1]
    hidden, rows = acts[0].shape[1:]
    block = features // 4
    specs, args = [], []
    for array in wide:
        for which in range(2):
            specs.append(pl.BlockSpec((rows, block), lambda i, p, which=which: (which, i)))
            args.append(array)
    return pl.pallas_call(
        functools.partial(grads_kernel, owned),
        grid_spec=pltpu.PrefetchScalarGridSpec(
            num_scalar_prefetch=1,
            grid=(features // block,),
            in_specs=specs + [pl.BlockSpec((3, hidden, rows), lambda i, p: (0, 0, 0))] * (owned + 1),
            out_specs=[pl.BlockSpec((owned, hidden, block), lambda i, p: (0, 0, i))] * 3,
        ),
        out_shape=[jax.ShapeDtypeStruct((owned, hidden, features), BF)] * 3,
        compiler_params=pltpu.CompilerParams(vmem_limit_bytes=56 * 1024 * 1024),
        name="weight_grads",
    )(pick, *args, *acts)


def hop(x, by):
    n = lax.axis_size("dp")
    return lax.ppermute(x, "dp", [(i, (i + 2 * by) % n) for i in range(n)])


def twin(x):
    return lax.ppermute(x, "dp", [(i, i ^ 1) for i in range(lax.axis_size("dp"))])


def spread(own):
    left, right = hop(own, 1), hop(own, -1)
    opp_in, opp_cot = hop(left[0], 1), hop(right[1], -1)
    mine = (own, right, left, opp_in, opp_cot)
    return (*mine, *(twin(piece) for piece in mine))


def gathered_sum(near, near_opp, far, far_opp):
    both_opp = (near_opp.astype(F32) + twin(far_opp).astype(F32)).astype(BF)
    both = near.astype(F32) + twin(far).astype(F32)
    from_left = hop(both_opp[0], 1).astype(F32)
    from_right = hop(both_opp[1], -1).astype(F32)
    to_right = jnp.stack([both[1, 0] + from_left, both[1, 1]]).astype(BF)
    to_left = jnp.stack([both[2, 0], both[2, 1] + from_right]).astype(BF)
    to_left, to_right = hop(to_left, -1), hop(to_right, 1)
    return (both[0] + to_right.astype(F32) + to_left.astype(F32)).astype(BF)


def body(tokens, cotangent, route, gate_prob, replica_pick, w_gate, w_up, w_down):
    groups = lax.axis_size("expert")
    column = lax.axis_index("expert")
    tok_dev, width = tokens.shape
    fanout = route.shape[1]
    owned = w_gate.shape[0]
    local_copies = owned + 1
    capacity = tok_dev * fanout // (groups * local_copies) + 2
    sizes = (owned, groups, capacity)
    rows = groups * capacity
    route_t, gate_t = route.T, gate_prob.T
    code, sends = send_rows(route_t, gate_t, tokens, cotangent, *sizes)

    own_pick = replica_pick[(column + groups // 2) % groups]
    place = lax.axis_index("dp")
    steps = jnp.array([0, 1, 3, 2, 0, 1, 3, 2, 0], jnp.int32)
    flip = jnp.array([0, 0, 0, 0, 1, 1, 1, 1, 0], jnp.int32)
    at = 2 * ((place // 2 + steps) % 4) + (place % 2 + flip) % 2
    at = jnp.where(jnp.arange(9) == 8, own_pick, at * width).astype(jnp.int32)

    def swap(x):
        x = x.reshape(groups, -1, width)
        return lax.all_to_all(x, "expert", split_axis=0, concat_axis=0, tiled=True)

    wide, acts, got = [], [], []
    for part, send in enumerate(sends):
        thin = swap(send).reshape(groups, 2, capacity, width).transpose(1, 0, 2, 3)
        if part == 1:
            pieces = spread(thin.reshape(2, rows, width))
            whole, act, *sums = ring_math(at, pieces, (w_gate, w_up, w_down), part, owned)
            wide.append(whole.reshape(2 * rows, -1))
        else:
            wide.append(lax.all_gather(thin.reshape(2 * rows, width), "dp", axis=1, tiled=True))
            act, *sums = expert_math(at, wide[part], (w_gate, w_up, w_down), part, owned, width)
        acts.append(act)
        back = gathered_sum(*sums)
        back = back.reshape(2, groups, capacity, width).transpose(1, 0, 2, 3)
        got.append(swap(back).reshape(groups * 2 * capacity, width))
    carried = ()
    for part in range(local_copies):
        carried = combine(code, gate_t, cotangent, got[part], carried, part, part == owned, *sizes)
    layer_out, token_grad, gate_part = carried
    gate_grad = lax.all_to_all(
        gate_part.reshape(fanout, 1, tok_dev), "dp", split_axis=0, concat_axis=0, tiled=True
    ).sum(axis=0)

    w_gate_grad, w_up_grad, w_down_grad = grads(
        own_pick.reshape(1), wide, acts, owned
    )
    return (layer_out, token_grad, gate_grad.reshape(tok_dev, 1), w_gate_grad, w_up_grad, w_down_grad)


def solution(mesh):
    in_specs = (
        P("expert", "dp"),
        P("expert", "dp"),
        P("expert", None),
        P("expert", None),
        P(),
        P("expert", "dp", None),
        P("expert", "dp", None),
        P("expert", "dp", None),
    )
    out_specs = (
        P("expert", "dp"),
        P("expert", "dp"),
        P("expert", "dp"),
        P("expert", "dp", None),
        P("expert", "dp", None),
        P("expert", "dp", None),
    )

    return jax.shard_map(body, mesh=mesh, in_specs=in_specs, out_specs=out_specs, check_vma=False)
```

```python
import functools

import jax
import jax.numpy as jnp
from jax import lax
from jax.experimental import pallas as pl
from jax.experimental.pallas import tpu as pltpu
from jax.sharding import PartitionSpec as P


BF = jnp.bfloat16
F32 = jnp.float32


def row_codes(first, rows, tok_dev, part, groups, owned, capacity):
    local_copies = owned + 1
    r = first + lax.broadcasted_iota(jnp.int32, (rows, tok_dev), 0)
    wide = 2 * capacity
    group = (r.astype(F32) * (1.0 / wide) + 0.5 / wide).astype(jnp.int32)
    inside = r - group * wide
    front = inside < capacity
    place = jnp.where(front, inside, inside - capacity)
    if part < owned:
        copy = group * local_copies + part
    else:
        holder = group + groups // 2
        holder = jnp.where(holder >= groups, holder - groups, holder)
        copy = holder * local_copies + owned
    return copy * capacity + place, front


def send_kernel(owned, groups, capacity, block, route_ref, gate_ref, tok_ref, cot_ref, code_ref, *out_refs):
    fanout, tok_dev = route_ref.shape
    copies = groups * (owned + 1)
    ids = lax.broadcasted_iota(jnp.int32, (copies, tok_dev), 0)
    named = jnp.zeros((copies, tok_dev), F32)
    for k in range(fanout):
        named = jnp.where(route_ref[k : k + 1, :] == ids, 1.0, named)
    before = lax.broadcasted_iota(jnp.int32, (tok_dev, tok_dev), 0) < lax.broadcasted_iota(
        jnp.int32, (tok_dev, tok_dev), 1
    )
    rank = jnp.dot(named.astype(BF), jnp.where(before, 1.0, 0.0).astype(BF), preferred_element_type=F32)
    codes, gates = [], []
    for k in range(fanout):
        row = route_ref[k : k + 1, :]
        at = jnp.sum(jnp.where(row == ids, rank, 0.0), axis=0, keepdims=True)
        codes.append(row * capacity + at.astype(jnp.int32))
        gates.append(gate_ref[k : k + 1, :])
    code_ref[...] = jnp.concatenate(codes, axis=0)
    both = jnp.concatenate([tok_ref[...], cot_ref[...]], axis=0)
    for part, out_ref in enumerate(out_refs):
        @pl.loop(0, 2)
        def _(half, part=part, out_ref=out_ref):
          for base in range(0, out_ref.shape[0] // 2, block):
            first = pl.multiple_of(half * (out_ref.shape[0] // 2) + base, block)
            slot, front = row_codes(first, block, tok_dev, part, groups, owned, capacity)
            match = jnp.zeros((block, tok_dev), F32)
            scale = jnp.zeros((block, tok_dev), F32)
            for k in range(fanout):
                same = codes[k] == slot
                match = jnp.where(same, 1.0, match)
                scale = jnp.where(same, gates[k], scale)
            pick = jnp.concatenate([jnp.where(front, match, 0.0), jnp.where(front, 0.0, match)], axis=1)
            rows = jnp.dot(pick.astype(BF), both, preferred_element_type=F32)
            scale = jnp.sum(jnp.where(front, 0.0, scale), axis=1, keepdims=True)
            scale = jnp.where(front[:, :1], 1.0, scale)
            out_ref[pl.ds(first, block), :] = (rows * scale).astype(BF)


def send_rows(route_t, gate_t, tokens, cot, owned, groups, capacity):
    rows, width = groups * 2 * capacity, tokens.shape[1]
    out = pl.pallas_call(
        functools.partial(send_kernel, owned, groups, capacity, 4 * 2 * capacity),
        out_shape=[jax.ShapeDtypeStruct(route_t.shape, jnp.int32)]
        + [jax.ShapeDtypeStruct((rows, width), BF)] * (owned + 1),
        name="send_rows",
    )(route_t, gate_t, tokens, cot)
    return out[0], out[1:]


def combine_kernel(owned, groups, capacity, part, first_call, last_call, *refs):
    code_ref, gate_ref, cot_ref, got_ref = refs[:4]
    acc_ref, gp_ref = (None, None) if first_call else refs[4:6]
    outs = refs[4:] if first_call else refs[6:]
    fanout, tok_dev = code_ref.shape
    nt = (((1,), (1,)), ((), ()))
    tn = (((0,), (0,)), ((), ()))
    block = 8 * 2 * capacity

    def step(i, carried):
        acc, gp = carried
        first = pl.multiple_of(i * block, block)
        got = got_ref[pl.ds(first, block), :]
        z = lax.dot_general(got, cot_ref[...], nt, preferred_element_type=F32)
        slot, front = row_codes(first, block, tok_dev, part, groups, owned, capacity)
        match = jnp.zeros(z.shape, F32)
        scale = jnp.zeros(z.shape, F32)
        zf = jnp.where(front, z, 0.0)
        parts = []
        for k in range(fanout):
            same = code_ref[k : k + 1, :] == slot
            match = jnp.where(same, 1.0, match)
            scale = jnp.where(same, gate_ref[k : k + 1, :], scale)
            parts.append(jnp.sum(jnp.where(same, zf, 0.0), axis=0, keepdims=True))
        scale = jnp.where(front, scale, 0.0)
        high = scale.astype(BF)
        low = (scale - high.astype(F32)).astype(BF)
        back = jnp.where(front, 0.0, match).astype(BF)
        weights = jnp.concatenate([high, low, back], axis=1)
        acc = acc + lax.dot_general(weights, got, tn, preferred_element_type=F32)
        return acc, gp + jnp.concatenate(parts, axis=0)

    start = (jnp.zeros((3 * tok_dev, cot_ref.shape[1]), F32), jnp.zeros((fanout, tok_dev), F32))
    acc, gp = lax.fori_loop(0, got_ref.shape[0] // block, step, start)
    if not first_call:
        acc = acc + acc_ref[...]
        gp = gp + gp_ref[...]
    if last_call:
        outs[0][...] = (acc[:tok_dev] + acc[tok_dev : 2 * tok_dev]).astype(BF)
        outs[1][...] = acc[2 * tok_dev :].astype(BF)
        outs[2][...] = gp
    else:
        outs[0][...] = acc
        outs[1][...] = gp


def combine(code, gate_t, cot, got, carried, part, last_call, owned, groups, capacity):
    tok_dev, width = cot.shape
    gp_shape = jax.ShapeDtypeStruct(code.shape, F32)
    if last_call:
        out_shape = [jax.ShapeDtypeStruct((tok_dev, width), BF)] * 2 + [gp_shape]
    else:
        out_shape = [jax.ShapeDtypeStruct((3 * tok_dev, width), F32), gp_shape]
    return pl.pallas_call(
        functools.partial(combine_kernel, owned, groups, capacity, part, not carried, last_call), out_shape=out_shape
    )(code, gate_t, cot, got, *carried)


def dot_nt(x, w):
    return lax.dot_general(x, w, (((1,), (1,)), ((), ())), preferred_element_type=F32)


def dot_nn(x, w):
    return jnp.dot(x, w, preferred_element_type=F32)


def write_rows(width, at_ref, acts, weights, outs):
    gate_ref, up_ref, down_ref = weights

    def rows_of(q):
        at = pl.ds(pl.multiple_of(at_ref[q], width), width)
        out = dot_nn(acts[0], down_ref[0, :, at])
        back = dot_nn(acts[1], gate_ref[0, :, at]) + dot_nn(acts[2], up_ref[0, :, at])
        return out.astype(BF), back.astype(BF)

    for side in range(2):
        near, opp = outs[2 * side], outs[2 * side + 1]

        @pl.loop(0, 3)
        def _(n, near=near, side=side):
            near[n, 0], near[n, 1] = rows_of(4 * side + n)

        opp[0], opp[1] = rows_of(4 * side + 3)


def math_kernel(width, at_ref, in_ref, cot_ref, gate_ref, up_ref, down_ref, acts_ref, *outs):
    gate_act = dot_nt(in_ref[...], gate_ref[0])
    up_act = dot_nt(in_ref[...], up_ref[0])
    d_hidden = dot_nt(cot_ref[...], down_ref[0])
    s = jax.nn.sigmoid(gate_act)
    activated = gate_act * s
    hidden = activated * up_act
    d_gate = d_hidden * up_act * s * (1.0 + gate_act * (1.0 - s))
    d_up = d_hidden * activated
    for n, act in enumerate((hidden, d_gate, d_up)):
        acts_ref[n] = act.T.astype(BF)
    hidden, d_gate, d_up = hidden.astype(BF), d_gate.astype(BF), d_up.astype(BF)
    acts = (hidden, d_gate, d_up)
    write_rows(width, at_ref, acts, (gate_ref, up_ref, down_ref), outs)


def expert_math(at, wide, weights, part, owned, width):
    rows = wide.shape[0] // 2
    hidden, features = weights[0].shape[1:]

    def whole(shape):
        return pl.BlockSpec(shape, lambda i, at: (0,) * len(shape))

    if part < owned:
        w_spec = pl.BlockSpec((1, hidden, features), lambda i, at: (part, 0, 0))
    else:
        w_spec = pl.BlockSpec((1, hidden, features), lambda i, at: (at[8], 0, 0))
    out_shape = [
        jax.ShapeDtypeStruct(shape, BF)
        for shape in (
            (3, hidden, rows),
            (3, 2, rows, width),
            (2, rows, width),
            (3, 2, rows, width),
            (2, rows, width),
        )
    ]
    return pl.pallas_call(
        functools.partial(math_kernel, width),
        grid_spec=pltpu.PrefetchScalarGridSpec(
            num_scalar_prefetch=1,
            grid=(1,),
            in_specs=[
                pl.BlockSpec((rows, features), lambda i, at: (0, 0)),
                pl.BlockSpec((rows, features), lambda i, at: (1, 0)),
            ]
            + [w_spec] * 3,
            out_specs=[whole(o.shape) for o in out_shape],
        ),
        out_shape=out_shape,
        compiler_params=pltpu.CompilerParams(vmem_limit_bytes=56 * 1024 * 1024),
    )(at, wide, wide, *weights)


def ring_math_kernel(width, at_ref, *refs):
    own, right, left, opp_in, opp_cot, p_own, p_side, p_opp = refs[:8]
    gate_ref, up_ref, down_ref, all_ref, acts_ref = refs[8:13]
    outs = refs[13:]

    def place(q):
        return pl.ds(pl.multiple_of(at_ref[q], width), width)

    for q, piece in ((0, own), (1, right), (2, left), (4, p_own), (5, p_side.at[0]), (6, p_side.at[1]), (7, p_opp)):
        all_ref[:, :, place(q)] = piece[...]
    all_ref[0, :, place(3)] = opp_in[...]
    all_ref[1, :, place(3)] = opp_cot[...]
    gate_act = dot_nt(all_ref[0], gate_ref[0])
    up_act = dot_nt(all_ref[0], up_ref[0])
    d_hidden = dot_nt(all_ref[1], down_ref[0])
    s = jax.nn.sigmoid(gate_act)
    activated = gate_act * s
    hidden = activated * up_act
    d_gate = d_hidden * up_act * s * (1.0 + gate_act * (1.0 - s))
    d_up = d_hidden * activated
    for n, act in enumerate((hidden, d_gate, d_up)):
        acts_ref[n] = act.T.astype(BF)
    hidden, d_gate, d_up = hidden.astype(BF), d_gate.astype(BF), d_up.astype(BF)
    acts = (hidden, d_gate, d_up)
    write_rows(width, at_ref, acts, (gate_ref, up_ref, down_ref), outs)


def ring_math(at, pieces, weights, part, owned):
    rows, width = pieces[3].shape
    features = weights[0].shape[2]
    hidden = weights[0].shape[1]

    def whole(shape):
        return pl.BlockSpec(shape, lambda i, at: (0,) * len(shape))

    if part < owned:
        w_spec = pl.BlockSpec((1, hidden, features), lambda i, at: (part, 0, 0))
    else:
        w_spec = pl.BlockSpec((1, hidden, features), lambda i, at: (at[8], 0, 0))
    out_shape = [
        jax.ShapeDtypeStruct(shape, BF)
        for shape in (
            (2, rows, features),
            (3, hidden, rows),
            (3, 2, rows, width),
            (2, rows, width),
            (3, 2, rows, width),
            (2, rows, width),
        )
    ]
    return pl.pallas_call(
        functools.partial(ring_math_kernel, width),
        grid_spec=pltpu.PrefetchScalarGridSpec(
            num_scalar_prefetch=1,
            grid=(1,),
            in_specs=[whole(p.shape) for p in pieces] + [w_spec] * 3,
            out_specs=[whole(o.shape) for o in out_shape],
        ),
        out_shape=out_shape,
        compiler_params=pltpu.CompilerParams(vmem_limit_bytes=56 * 1024 * 1024),
    )(at, *pieces, *weights)


def grads_kernel(owned, pick_ref, *refs):
    n_parts = owned + 1
    wide, acts, outs = refs[: 2 * n_parts], refs[2 * n_parts : 3 * n_parts], refs[3 * n_parts :]
    for out_ref, n, which in zip(outs, (1, 2, 0), (0, 0, 1)):
        extra = dot_nn(acts[owned][n], wide[2 * owned + which][...])
        for i in range(owned):
            keep = jnp.where(pick_ref[0] == i, 1.0, 0.0)
            out_ref[i] = (dot_nn(acts[i][n], wide[2 * i + which][...]) + keep * extra).astype(BF)


def grads(pick, wide, acts, owned):
    features = wide[0].shape[1]
    hidden, rows = acts[0].shape[1:]
    block = features // 4
    specs, args = [], []
    for array in wide:
        for which in range(2):
            specs.append(pl.BlockSpec((rows, block), lambda i, p, which=which: (which, i)))
            args.append(array)
    return pl.pallas_call(
        functools.partial(grads_kernel, owned),
        grid_spec=pltpu.PrefetchScalarGridSpec(
            num_scalar_prefetch=1,
            grid=(features // block,),
            in_specs=specs + [pl.BlockSpec((3, hidden, rows), lambda i, p: (0, 0, 0))] * (owned + 1),
            out_specs=[pl.BlockSpec((owned, hidden, block), lambda i, p: (0, 0, i))] * 3,
        ),
        out_shape=[jax.ShapeDtypeStruct((owned, hidden, features), BF)] * 3,
        compiler_params=pltpu.CompilerParams(vmem_limit_bytes=56 * 1024 * 1024),
        name="weight_grads",
    )(pick, *args, *acts)


def hop(x, by):
    n = lax.axis_size("dp")
    return lax.ppermute(x, "dp", [(i, (i + 2 * by) % n) for i in range(n)])


def twin(x):
    return lax.ppermute(x, "dp", [(i, i ^ 1) for i in range(lax.axis_size("dp"))])


def spread(own):
    left, right = hop(own, 1), hop(own, -1)
    opp_in, opp_cot = hop(left[0], 1), hop(right[1], -1)
    theirs = (own, jnp.stack([right, left]), jnp.stack([opp_in, opp_cot]))
    return (own, right, left, opp_in, opp_cot, *(twin(piece) for piece in theirs))


def gathered_sum(near, near_opp, far, far_opp):
    both_opp = (near_opp.astype(F32) + twin(far_opp).astype(F32)).astype(BF)
    both = near.astype(F32) + twin(far).astype(F32)
    from_left = hop(both_opp[0], 1).astype(F32)
    from_right = hop(both_opp[1], -1).astype(F32)
    to_right = jnp.stack([both[1, 0] + from_left, both[1, 1]]).astype(BF)
    to_left = jnp.stack([both[2, 0], both[2, 1] + from_right]).astype(BF)
    to_left, to_right = hop(to_left, -1), hop(to_right, 1)
    return (both[0] + to_right.astype(F32) + to_left.astype(F32)).astype(BF)


def body(tokens, cotangent, route, gate_prob, replica_pick, w_gate, w_up, w_down):
    groups = lax.axis_size("expert")
    column = lax.axis_index("expert")
    tok_dev, width = tokens.shape
    fanout = route.shape[1]
    owned = w_gate.shape[0]
    local_copies = owned + 1
    capacity = tok_dev * fanout // (groups * local_copies) + 2
    sizes = (owned, groups, capacity)
    rows = groups * capacity
    route_t, gate_t = route.T, gate_prob.T
    code, sends = send_rows(route_t, gate_t, tokens, cotangent, *sizes)

    own_pick = replica_pick[(column + groups // 2) % groups]
    place = lax.axis_index("dp")
    steps = jnp.array([0, 1, 3, 2, 0, 1, 3, 2, 0], jnp.int32)
    flip = jnp.array([0, 0, 0, 0, 1, 1, 1, 1, 0], jnp.int32)
    at = 2 * ((place // 2 + steps) % 4) + (place % 2 + flip) % 2
    at = jnp.where(jnp.arange(9) == 8, own_pick, at * width).astype(jnp.int32)

    def swap(x):
        x = x.reshape(groups, -1, width)
        return lax.all_to_all(x, "expert", split_axis=0, concat_axis=0, tiled=True)

    wide, acts, got = [], [], []
    for part, send in enumerate(sends):
        thin = swap(send).reshape(groups, 2, capacity, width).transpose(1, 0, 2, 3)
        if part == 1:
            pieces = spread(thin.reshape(2, rows, width))
            whole, act, *sums = ring_math(at, pieces, (w_gate, w_up, w_down), part, owned)
            wide.append(whole.reshape(2 * rows, -1))
        else:
            wide.append(lax.all_gather(thin.reshape(2 * rows, width), "dp", axis=1, tiled=True))
            act, *sums = expert_math(at, wide[part], (w_gate, w_up, w_down), part, owned, width)
        acts.append(act)
        back = gathered_sum(*sums)
        back = back.reshape(2, groups, capacity, width).transpose(1, 0, 2, 3)
        got.append(swap(back).reshape(groups * 2 * capacity, width))
    carried = ()
    for part in range(local_copies):
        carried = combine(code, gate_t, cotangent, got[part], carried, part, part == owned, *sizes)
    layer_out, token_grad, gate_part = carried
    gate_grad = lax.all_to_all(
        gate_part.reshape(fanout, 1, tok_dev), "dp", split_axis=0, concat_axis=0, tiled=True
    ).sum(axis=0)

    w_gate_grad, w_up_grad, w_down_grad = grads(
        own_pick.reshape(1), wide, acts, owned
    )
    return (layer_out, token_grad, gate_grad.reshape(tok_dev, 1), w_gate_grad, w_up_grad, w_down_grad)


def solution(mesh):
    in_specs = (
        P("expert", "dp"),
        P("expert", "dp"),
        P("expert", None),
        P("expert", None),
        P(),
        P("expert", "dp", None),
        P("expert", "dp", None),
        P("expert", "dp", None),
    )
    out_specs = (
        P("expert", "dp"),
        P("expert", "dp"),
        P("expert", "dp"),
        P("expert", "dp", None),
        P("expert", "dp", None),
        P("expert", "dp", None),
    )

    return jax.shard_map(body, mesh=mesh, in_specs=in_specs, out_specs=out_specs, check_vma=False)
```
